128 devices in a mesh: leaf: 16 (over x, z), sub: 8 (over y, core).
Axes of the slice: x: 4, y: 4, z: 4, core: 2. Of those that a mesh axis runs over, the one named last changes fastest.
Arguments:
- beads: float32 [262144, 128], P(('leaf', 'sub')), may hold values from -6 to 6
- rot_perm: int32 [262144], P(('leaf', 'sub')), may hold values from 0 to 262143, as said below
- pool_ids: int32 [262144], P(('leaf', 'sub')), may hold values from 0 to 32767, as said below
- ball_counts: int32 [16, 8], P('leaf'), may hold values from 1 to 24, 64 in all within a row
- fine_qkv: bfloat16 [2, 128, 384], replicated
- fine_out: bfloat16 [2, 128, 128], replicated, may hold values from -0.5 to 0.5
- pool_weight: bfloat16 [1024, 512], replicated, may hold values from -0.1875 to 0.1875
- coarse_qkv: bfloat16 [2, 512, 1536], replicated
- coarse_out: bfloat16 [2, 512, 512], replicated, may hold values from -0.25 to 0.25
- unpool_weight: bfloat16 [512, 1024], replicated, may hold values from -0.25 to 0.25
Outputs:
- denoised: float32 [262144, 128], P(('leaf', 'sub'))
The draws below stay inside these ranges and needn't reach their ends.
Inputs may be any that keep to these rules, and one draw needn't show every extreme that they name: `rot_perm`: a permutation of all 262144 beads; the 2048 rotated-order positions of each device name exactly 16 beads of every device, devices counted in the order of the arrays' rows. `pool_ids`: the 2048 beads of the device in row block d fall into 256 groups of exactly eight, numbered d * 256 to (d + 1) * 256 - 1. `ball_counts`: each row sums to 64.
All inputs are finite; a program needn't handle non-finite values.
Results may differ from the reference program's by a relative error of at most 0.017.
The reference program's roundings to bfloat16 on the way count: a program that leaves them out, or rounds other values in their place, can miss the bound.
Values may be sent and summed in bfloat16 or wider, within the bound.
No kernel may reach another device: no remote copies, remote signals or barrier semaphores. Data moves between devices by JAX's collectives and lax.ppermute only.
A program may use at most 128 MiB of HBM per device.

```python
import math
import jax
import jax.numpy as jnp
import numpy as np
from jax import lax

WIDTH = 128
HEADS = 4
CWIDTH = 512
CHEADS = 8
BALL = 256
GRAN = 32
BEADS_DEV = 2048
BEADS = 262144
POOLED_DEV = 256
POOLED = 32768
BLOCKS_DEV = 8
MOST_BLOCKS = 24
N_LEAF = 16
N_SUB = 8


def draw_rot_perm(key, part):
    devices = BEADS // BEADS_DEV
    bucket = BEADS_DEV // devices

    def own_order(device_index):
        ordering = jax.random.permutation(jax.random.fold_in(key, device_index), BEADS_DEV).astype(jnp.int32)
        return ordering + device_index * BEADS_DEV
    sources = jax.vmap(own_order)(jnp.arange(devices, dtype=jnp.int32))
    routed = sources.reshape(devices, devices, bucket).transpose(1, 0, 2).reshape(devices, BEADS_DEV)

    def shuffle(device_index, routed_row):
        ordering = jax.random.permutation(jax.random.fold_in(jax.random.fold_in(key, 977), device_index), BEADS_DEV)
        return routed_row[ordering]
    shuffled = jax.vmap(shuffle)(jnp.arange(devices, dtype=jnp.int32), routed)
    return shuffled.reshape(BEADS).astype(jnp.int32)


def draw_pool_ids(key, part):
    devices = BEADS // BEADS_DEV

    def own_groups(device_index):
        ordering = jax.random.permutation(jax.random.fold_in(key, device_index + 31), BEADS_DEV).astype(jnp.int32)
        return ordering // 8 + device_index * POOLED_DEV
    return jax.vmap(own_groups)(jnp.arange(devices, dtype=jnp.int32)).reshape(BEADS).astype(jnp.int32)


def scaled_projection(key, channels):
    initial = jax.random.normal(key, (2, channels, 3 * channels), jnp.float32) / math.sqrt(channels)
    return initial.astype(jnp.bfloat16)


def draw_fine_qkv(key, part):
    return scaled_projection(key, WIDTH)


def draw_coarse_qkv(key, part):
    return scaled_projection(key, CWIDTH)


def block_scale(rng, shape, shards, smallest, top_value):
    def one(axis_at, shards_of):
        heights = jax.random.uniform(jax.random.fold_in(jax.random.fold_in(rng, 6), axis_at), (shards_of,), jnp.float32, smallest / len(shards), top_value / len(shards))
        return jnp.repeat(jnp.exp(heights), shape[axis_at] // shards_of).reshape((-1,) + (1,) * (len(shape) - axis_at - 1))

    factor_of = one(*shards[0])
    for cut in shards[1:]:
        factor_of = factor_of * one(*cut)
    return factor_of


def length_profile(number_of, total, limit, skew):
    portions = [(1 << 20) // math.isqrt(standing ** skew) + 1 for standing in range(2, number_of + 1)]
    rest, given = total - limit - (number_of - 1), [1] * (number_of - 1)
    while rest > 0:
        candidates = [i for i in range(number_of - 1) if given[i] < limit]
        whole, left = sum([portions[i] for i in candidates]), rest
        for i in candidates:
            extra = min(limit - given[i], max(1, left * portions[i] // whole), rest)
            given[i] = given[i] + extra
            rest = rest - extra
    return np.array([limit] + given)


def ragged(key, count, total, most, lean):
    if count == 2:
        one = jax.random.randint(key, (), max(1, total - most), min(most, total - 1) + 1)
        return jnp.stack([one, total - one])
    lengths = jnp.asarray(length_profile(count, total, most, lean), jnp.int32)
    pairs = (count - 1) // 2
    donor, taker = lengths[1:1 + 2 * pairs:2], lengths[2:2 + 2 * pairs:2]
    margin = jnp.minimum(donor - 1, most - taker)
    moved = jax.random.randint(jax.random.fold_in(key, 1), (pairs,), 0, 1 << 20) % (margin + 1)
    lengths = lengths.at[1:1 + 2 * pairs:2].set(donor - moved).at[2:2 + 2 * pairs:2].set(taker + moved)
    return lengths[jax.random.permutation(jax.random.fold_in(key, 2), count)]


def bell_draw(stream_key, dims, width, limit, shards=(), kind=jnp.bfloat16):
    values = width * jax.random.normal(stream_key, dims, jnp.float32)
    if shards:
        values = values * block_scale(stream_key, dims, shards, -0.22, 0.18)
    return jnp.clip(values, -limit, limit).astype(kind)


def setup_inputs(seed: int = 0) -> dict:
    seeds = jax.random.split(jax.random.key(seed), 11)
    return {
        "beads": bell_draw(seeds[0], (BEADS, WIDTH), 1.0, 6.0, ((0, 128),), jnp.float32),
        "rot_perm": draw_rot_perm(jax.random.fold_in(seeds[10], 71), 0),
        "pool_ids": draw_pool_ids(jax.random.fold_in(seeds[10], 71), 0),
        "ball_counts": jax.vmap(lambda own: ragged(own, N_SUB, N_SUB * BLOCKS_DEV, MOST_BLOCKS, 2))(jax.random.split(seeds[3], N_LEAF)).reshape((N_LEAF, N_SUB)).astype(jnp.int32),
        "fine_qkv": draw_fine_qkv(jax.random.fold_in(seeds[10], 71), 0),
        "fine_out": bell_draw(seeds[5], (2, WIDTH, WIDTH), WIDTH ** -0.5, 0.5),
        "pool_weight": bell_draw(seeds[6], (8 * WIDTH, CWIDTH), (8 * WIDTH) ** -0.5, 0.1875),
        "coarse_qkv": draw_coarse_qkv(jax.random.fold_in(seeds[10], 71), 0),
        "coarse_out": bell_draw(seeds[8], (2, CWIDTH, CWIDTH), CWIDTH ** -0.5, 0.25),
        "unpool_weight": bell_draw(seeds[9], (CWIDTH, 8 * WIDTH), CWIDTH ** -0.5, 0.25),
    }


def widen_rounded(values):
    return lax.optimization_barrier(values.astype(jnp.bfloat16)).astype(jnp.float32)

def layer_norm(features):
    centre = features - lax.optimization_barrier(jnp.mean(features, axis=-1, keepdims=True))
    spread = lax.optimization_barrier(jnp.mean(centre * centre, axis=-1, keepdims=True))
    return centre * lax.rsqrt(spread + 1e-05)

def ball_layer(features, qkv_weight, out_weight, head_count, ball_size):
    row_count, channels = features.shape
    head_size = channels // head_count
    normed = layer_norm(features).astype(jnp.bfloat16)
    projected = widen_rounded(jnp.dot(normed, qkv_weight, preferred_element_type=jnp.float32))
    shaped = projected.reshape(row_count // ball_size, ball_size, 3, head_count, head_size)
    scores = jnp.einsum('bqhd,bkhd->bhqk', shaped[:, :, 0], shaped[:, :, 1]) / math.sqrt(head_size)
    weights = widen_rounded(jax.nn.softmax(scores, axis=-1))
    attended = jnp.einsum('bhqk,bkhd->bqhd', weights, shaped[:, :, 2])
    attended = attended.astype(jnp.bfloat16).reshape(row_count, channels)
    return features + jnp.dot(attended, out_weight, preferred_element_type=jnp.float32)

def fine_pass(features, qkv_weight, out_weight):
    pieces = features.reshape(-1, BEADS_DEV, WIDTH)
    finished = lax.map(lambda one_block: ball_layer(one_block, qkv_weight, out_weight, HEADS, BALL), pieces)
    return finished.reshape(BEADS, WIDTH)

def coarse_layer(features, qkv_weight, out_weight, ball_of):
    row_count, channels = features.shape
    head_size = channels // CHEADS
    normed = layer_norm(features).astype(jnp.bfloat16)
    projected = widen_rounded(jnp.dot(normed, qkv_weight, preferred_element_type=jnp.float32))
    shaped = projected.reshape(row_count, 3, CHEADS, head_size)
    key_rows = shaped[:, 1]
    value_rows = shaped[:, 2]
    query_tiles = shaped[:, 0].reshape(-1, POOLED_DEV, CHEADS, head_size)
    tile_balls = ball_of.reshape(-1, POOLED_DEV)

    def one_tile(packed):
        tile_rows, tile_ball = packed
        scores = jnp.einsum('qhd,khd->hqk', tile_rows, key_rows) / math.sqrt(head_size)
        allowed = tile_ball[:, None] == ball_of[None, :]
        scores = jnp.where(allowed[None], scores, -1e+30)
        weights = widen_rounded(jax.nn.softmax(scores, axis=-1))
        return jnp.einsum('hqk,khd->qhd', weights, value_rows)
    attended = lax.map(one_tile, (query_tiles, tile_balls))
    attended = attended.astype(jnp.bfloat16).reshape(row_count, channels)
    return features + jnp.dot(attended, out_weight, preferred_element_type=jnp.float32)

def reference(beads, rot_perm, pool_ids, ball_counts, fine_qkv, fine_out, pool_weight, coarse_qkv, coarse_out, unpool_weight):
    after_tree = fine_pass(beads, fine_qkv[0], fine_out[0])
    rotated = fine_pass(after_tree[rot_perm], fine_qkv[1], fine_out[1])
    settled = jnp.zeros_like(after_tree).at[rot_perm].set(rotated)
    grouping = jnp.argsort(pool_ids, stable=True)
    gathered = settled[grouping].reshape(POOLED, 8 * WIDTH).astype(jnp.bfloat16)
    pooled = widen_rounded(jnp.dot(gathered, pool_weight, preferred_element_type=jnp.float32))
    groups = pooled.reshape(N_LEAF, N_SUB * POOLED_DEV, CWIDTH)

    def one_group(packed):
        features, counts = packed
        ball_ends = jnp.cumsum(counts)
        block_ids = jnp.arange(features.shape[0]) // GRAN
        ball_of = lax.optimization_barrier(jnp.sum(block_ids[:, None] >= ball_ends[None, :], axis=1))
        current = features
        for layer_index in range(2):
            current = coarse_layer(current, coarse_qkv[layer_index], coarse_out[layer_index], ball_of)
        return widen_rounded(current)
    coarse = lax.map(one_group, (groups, ball_counts)).reshape(POOLED, CWIDTH)
    expanded = jnp.dot(layer_norm(coarse).astype(jnp.bfloat16), unpool_weight, preferred_element_type=jnp.float32)
    spread_back = jnp.zeros_like(settled).at[grouping].set(expanded.reshape(BEADS, WIDTH))
    return settled + spread_back
```

```python
import functools
import math

import jax
import jax.numpy as jnp
from jax import lax
from jax.experimental import pallas as pl
from jax.experimental.pallas import tpu as pltpu
from jax.sharding import PartitionSpec as P

HEADS = 4
CHEADS = 8
BALL = 256
GRAN = 32
LOG2E = 1.4426950408889634
NEG = -1e30
F32 = jnp.float32
BF16 = jnp.bfloat16


def vmem():
    return pl.BlockSpec(memory_space=pltpu.VMEM)


def smem():
    return pl.BlockSpec(memory_space=pltpu.SMEM)


def dot(a, b, dims=((1,), (0,))):
    return lax.dot_general(a, b, (dims, ((), ())), preferred_element_type=F32)


def call(kernel, out_shape, in_specs, out_specs, scratch=(), flops=0, nbytes=0, name=None):
    return pl.pallas_call(
        kernel,
        out_shape=out_shape,
        in_specs=in_specs,
        out_specs=out_specs,
        scratch_shapes=list(scratch),
        cost_estimate=pl.CostEstimate(flops=flops, bytes_accessed=nbytes, transcendentals=0),
        name=name,
    )


def ranks(classes, of_ref, count, total):
    step = 256
    tri = (
        lax.broadcasted_iota(jnp.int32, (step, step), 0)
        <= lax.broadcasted_iota(jnp.int32, (step, step), 1)
    )
    tri = jnp.where(tri, 1.0, 0.0).astype(BF16)
    names = lax.broadcasted_iota(jnp.int32, (count, step), 0)
    carried = jnp.zeros((count, 1), F32)
    hots, found = [], []
    for row in range(total // step):
        hot = jnp.where(names == classes[row], 1.0, 0.0)
        hot16 = hot.astype(BF16)
        running = dot(hot16, tri) + carried
        found.append(jnp.sum(hot * running, axis=0, keepdims=True) - 1.0)
        hots.append(hot16)
        carried = running[:, step - 1 : step]
    return hots, found


def route_kernel(rot_ref, wanted_ref, slot_ref, *, own, devices):
    rows = own // 256
    bucket = own // devices
    dest = [rot_ref[r : r + 1, :] // own for r in range(rows)]
    hots, found = ranks(dest, rot_ref, devices, own)
    lanes = lax.broadcasted_iota(jnp.int32, (bucket, 256), 0)
    total = jnp.zeros((devices, 2 * bucket), F32)
    for r in range(rows):
        rank = found[r].astype(jnp.int32)
        slot_ref[r : r + 1, :] = dest[r] * bucket + rank
        local = rot_ref[r : r + 1, :] % own
        here = lanes == rank
        high = jnp.where(here, (local // 64).astype(F32), 0.0)
        low = jnp.where(here, (local % 64).astype(F32), 0.0)
        parts = jnp.concatenate([high, low], axis=0).astype(BF16)
        total = total + dot(hots[r], parts, ((1,), (1,)))
    wanted = total[:, :bucket] * 64.0 + total[:, bucket:]
    wanted_ref[...] = jnp.zeros_like(wanted_ref)
    wanted_ref[:, :bucket] = wanted.astype(jnp.int32)


def place_kernel(pool_ref, place_ref, *, own, nodes):
    rows = own // 256
    node = [pool_ref[r : r + 1, :] % nodes for r in range(rows)]
    _, found = ranks(node, pool_ref, nodes, own)
    for r in range(rows):
        place_ref[r : r + 1, :] = found[r].astype(jnp.int32) * nodes + node[r]


def norm_rows(x):
    centre = x - jnp.mean(x, axis=-1, keepdims=True)
    spread = jnp.mean(centre * centre, axis=-1, keepdims=True)
    return (centre * lax.rsqrt(spread + 1e-5)).astype(BF16)


def norm_columns(x):
    centre = x - jnp.mean(x, axis=0, keepdims=True)
    spread = jnp.mean(centre * centre, axis=0, keepdims=True)
    return (centre * lax.rsqrt(spread + 1e-5)).astype(BF16)


def ball(x, key_weight, qv_weight, out_weight):
    rows, channels = x.shape
    size = channels // HEADS
    normed = norm_rows(x)
    keys = dot(normed, key_weight).astype(BF16)
    qv = dot(qv_weight, normed, ((1,), (1,))).astype(BF16)
    ones = jnp.ones((16, rows), BF16)
    attended = []
    for head in range(HEADS):
        mine = slice(head * size, (head + 1) * size)
        above, below = head * size, channels - (head + 1) * size
        pieces = [qv[mine]]
        if above:
            pieces = [jnp.zeros((above, rows), BF16)] + pieces
        if below:
            pieces = pieces + [jnp.zeros((below, rows), BF16)]
        queries = jnp.concatenate(pieces, axis=0)
        scores = dot(keys, queries)
        most = jnp.max(scores, axis=0, keepdims=True)
        weights = jnp.exp2((scores - most) * (LOG2E / math.sqrt(size))).astype(BF16)
        values = jnp.concatenate([qv[channels + head * size : channels + (head + 1) * size], ones], 0)
        summed = dot(values, weights)
        attended.append((summed[:size] / summed[size : size + 1]).astype(BF16))
    attended = jnp.concatenate(attended, axis=0)
    return x + dot(attended, out_weight, ((0,), (0,)))


def first_kernel(x_ref, key_ref, qv_ref, out_ref, y_ref):
    def one(at, _):
        rows = pl.ds(pl.multiple_of(at * BALL, BALL), BALL)
        y_ref[rows, :] = ball(x_ref[rows, :], key_ref[...], qv_ref[...], out_ref[...])
        return 0

    lax.fori_loop(0, x_ref.shape[0] // BALL, one, 0)


def answer_kernel(wanted_ref, x_ref, out_ref, rows_ref, *, bucket):
    def one(device, _):
        for j in range(bucket):
            rows_ref[pl.ds(device * bucket + j, 1), :] = x_ref[pl.ds(wanted_ref[device, j], 1), :]
        return 0

    lax.fori_loop(0, wanted_ref.shape[0], one, 0)
    out_ref[...] = rows_ref[...].astype(BF16)


def second_kernel(slot_ref, x_ref, key_ref, qv_ref, out_ref, y_ref, from_ref, to_ref, ball_ref):
    from_ref[...] = x_ref[...].astype(F32)

    def one(at, _):
        def take(step, _):
            for j in range(16):
                row = step * 16 + j
                ball_ref[pl.ds(row, 1), :] = from_ref[pl.ds(slot_ref[at, row], 1), :]
            return 0

        lax.fori_loop(0, BALL // 16, take, 0)
        ball_ref[...] = ball(ball_ref[...], key_ref[...], qv_ref[...], out_ref[...])

        def give(step, _):
            for j in range(16):
                row = step * 16 + j
                to_ref[pl.ds(slot_ref[at, row], 1), :] = ball_ref[pl.ds(row, 1), :]
            return 0

        lax.fori_loop(0, BALL // 16, give, 0)
        return 0

    lax.fori_loop(0, x_ref.shape[0] // BALL, one, 0)
    y_ref[...] = to_ref[...].astype(BF16)


def send_projected(features, weight_ref, message_ref):
    normed = norm_columns(features)
    channels = features.shape[0]
    size = channels // CHEADS
    for part in range(3):
        projected = dot(weight_ref[part * channels : (part + 1) * channels, :], normed).astype(BF16)
        for head in range(CHEADS):
            message_ref[head, part * size : (part + 1) * size, :] = projected[
                head * size : (head + 1) * size
            ]


def pool_kernel(
    wanted_ref, place_ref, x_ref, pool_ref, qkv_ref, message_ref, pooled_ref, placed_ref, from_ref, *, bucket
):
    from_ref[...] = x_ref[...].astype(F32)

    def one(device, _):
        for j in range(bucket):
            bead = wanted_ref[device, j]
            placed_ref[pl.ds(place_ref[bead // 256, bead % 256], 1), :] = from_ref[
                pl.ds(device * bucket + j, 1), :
            ]
        return 0

    lax.fori_loop(0, wanted_ref.shape[0], one, 0)
    nodes = x_ref.shape[0] // 8
    channels = x_ref.shape[1]
    pooled = None
    for k in range(8):
        part = dot(
            pool_ref[:, k * channels : (k + 1) * channels],
            placed_ref[k * nodes : (k + 1) * nodes, :].astype(BF16),
            ((1,), (1,)),
        )
        pooled = part if pooled is None else pooled + part
    pooled = pooled.astype(BF16).astype(F32)
    pooled_ref[...] = pooled
    send_projected(pooled, qkv_ref, message_ref)


def coarse_kernel(counts_ref, x_ref, out_ref, keys_ref, of_ref, first_ref, last_ref):
    tiles, parts, width = x_ref.shape
    size = parts // 3
    balls = counts_ref.shape[1]
    per_tile = width // GRAN
    for t in range(tiles):
        keys_ref[t] = x_ref[t, size : 2 * size, :].astype(F32).T.astype(BF16)
    start = 0
    ends = []
    for e in range(balls):
        end = start + counts_ref[0, e]

        def mark(block, _, e=e, start=start, end=end):
            of_ref[block] = e
            first_ref[block] = start
            last_ref[block] = end - 1
            return 0

        lax.fori_loop(start, end, mark, 0)
        ends.append(end)
        start = end
    ones = jnp.ones((16, width), BF16)

    def one(tile, _):
        queries = x_ref[tile, :size, :]
        blocks = tile * per_tile + lax.broadcasted_iota(jnp.int32, (1, width), 1) // GRAN
        own = jnp.zeros((1, width), jnp.int32)
        for e in range(balls):
            own = own + jnp.where(blocks >= ends[e], 1, 0)
        low = first_ref[tile * per_tile] // per_tile
        high = last_ref[tile * per_tile + per_tile - 1] // per_tile

        def add(chunk, carry):
            most, total = carry
            scores = dot(keys_ref[chunk], queries)
            masked = []
            for g in range(per_tile):
                seen = own == of_ref[chunk * per_tile + g]
                masked.append(jnp.where(seen, scores[g * GRAN : (g + 1) * GRAN], NEG))
            scores = jnp.concatenate(masked, axis=0)
            now = jnp.maximum(most, jnp.max(scores, axis=0, keepdims=True))
            scale = LOG2E / math.sqrt(size)
            weights = jnp.exp2((scores - now) * scale).astype(BF16)
            values = jnp.concatenate([x_ref[chunk, 2 * size :, :], ones], axis=0)
            return now, total * jnp.exp2((most - now) * scale) + dot(values, weights)

        begin = (jnp.full((1, width), NEG, F32), jnp.zeros((size + 16, width), F32))
        _, total = lax.fori_loop(low, high + 1, add, begin)
        out_ref[tile] = (total[:size] / total[size : size + 1]).astype(BF16)
        return 0

    lax.fori_loop(0, tiles, one, 0)


def between_kernel(x_ref, features_ref, out_weight_ref, qkv_ref, message_ref, next_ref):
    heads, size, width = x_ref.shape
    features = features_ref[...] + dot(out_weight_ref[...], x_ref[...].reshape(heads * size, width))
    next_ref[...] = features
    send_projected(features, qkv_ref, message_ref)


def last_kernel(place_ref, x_ref, features_ref, out_weight_ref, unpool_ref, placed_ref, out_ref, sum_ref):
    heads, size, width = x_ref.shape
    features = features_ref[...] + dot(out_weight_ref[...], x_ref[...].reshape(heads * size, width))
    features = features.astype(BF16).astype(F32)
    normed = norm_columns(features).astype(F32).T.astype(BF16)
    channels = placed_ref.shape[1]
    for k in range(8):
        rows = slice(k * width, (k + 1) * width)
        expanded = dot(normed, unpool_ref[:, k * channels : (k + 1) * channels])
        sum_ref[rows, :] = placed_ref[rows, :] + expanded

    def one(step, _):
        for j in range(16):
            row = step * 16 + j
            out_ref[pl.ds(row, 1), :] = sum_ref[pl.ds(place_ref[row // 256, row % 256], 1), :]
        return 0

    lax.fori_loop(0, out_ref.shape[0] // 16, one, 0)


def shaped(shape, dtype):
    return jax.ShapeDtypeStruct(shape, dtype)


def exchange(value, axes):
    return lax.all_to_all(value, axes, split_axis=0, concat_axis=0, tiled=True)


def shards(
    beads,
    rot_perm,
    pool_ids,
    ball_counts,
    fine_qkv,
    fine_out,
    pool_weight,
    coarse_qkv,
    coarse_out,
    unpool_weight,
):
    own, channels = beads.shape
    both = ("leaf", "sub")
    subs = lax.axis_size("sub")
    devices = lax.axis_size("leaf") * subs
    bucket = own // devices
    nodes = own // 8
    wide = pool_weight.shape[1]
    size = wide // CHEADS
    rows = own // 256

    wanted, slots = call(
        functools.partial(route_kernel, own=own, devices=devices),
        (shaped((devices, 128), jnp.int32), shaped((rows, 256), jnp.int32)),
        [vmem()],
        (vmem(), vmem()),
        flops=2 * devices * own * 256,
        nbytes=100000,
        name="route",
    )(rot_perm.reshape(rows, 256))
    requested = exchange(wanted.reshape(devices, 1, 128), both).reshape(devices, 128)
    places = call(
        functools.partial(place_kernel, own=own, nodes=nodes),
        shaped((rows, 256), jnp.int32),
        [vmem()],
        vmem(),
        flops=2 * nodes * own * 256,
        nbytes=20000,
        name="place",
    )(pool_ids.reshape(rows, 256))

    key_weights = fine_qkv[:, :, channels : 2 * channels]
    qv_weights = jnp.concatenate(
        [fine_qkv[:, :, :channels], fine_qkv[:, :, 2 * channels :]], axis=2
    ).transpose(0, 2, 1)
    pool_turned = pool_weight.T
    coarse_turned = coarse_qkv.transpose(0, 2, 1)
    out_turned = coarse_out.transpose(0, 2, 1)
    ball_flops = own * channels * channels * 8 + own * BALL * channels * 16

    after_tree = call(
        first_kernel,
        shaped((own, channels), F32),
        [vmem()] * 4,
        vmem(),
        flops=ball_flops,
        nbytes=own * channels * 8,
        name="first",
    )(beads, key_weights[0], qv_weights[0], fine_out[0])
    answer = call(
        functools.partial(answer_kernel, bucket=bucket),
        shaped((own, channels), BF16),
        [smem(), vmem()],
        vmem(),
        [pltpu.VMEM((own, channels), F32)],
        nbytes=own * channels * 6,
        name="answer",
    )(requested, after_tree)
    arrived = exchange(answer.reshape(devices, bucket, channels), both).reshape(own, channels)
    outgoing = call(
        second_kernel,
        shaped((own, channels), BF16),
        [smem()] + [vmem()] * 4,
        vmem(),
        [pltpu.VMEM((own, channels), F32)] * 2 + [pltpu.VMEM((BALL, channels), F32)],
        flops=ball_flops,
        nbytes=own * channels * 4,
        name="second",
    )(slots, arrived, key_weights[1], qv_weights[1], fine_out[1])
    coming = exchange(outgoing.reshape(devices, bucket, channels), both).reshape(own, channels)
    message, features, placed = call(
        functools.partial(pool_kernel, bucket=bucket),
        (
            shaped((CHEADS, 3 * size, nodes), BF16),
            shaped((wide, nodes), F32),
            shaped((own, channels), F32),
        ),
        [smem(), smem()] + [vmem()] * 3,
        (vmem(), vmem(), vmem()),
        [pltpu.VMEM((own, channels), F32)],
        flops=2 * nodes * wide * (own // 2 + 3 * wide),
        nbytes=own * channels * 8,
        name="pool",
    )(requested, places, coming, pool_turned, coarse_turned[0])
    for layer in range(2):
        received = exchange(message, "sub")
        attended = call(
            coarse_kernel,
            shaped((subs, size, nodes), BF16),
            [smem(), vmem()],
            vmem(),
            [pltpu.VMEM((subs, nodes, size), BF16)] + [pltpu.SMEM((subs * nodes // GRAN,), jnp.int32)] * 3,
            flops=subs * nodes * nodes * 3 * size * 4,
            nbytes=subs * nodes * size * 8,
            name="coarse",
        )(ball_counts, received)
        back = exchange(attended, "sub")
        if layer == 0:
            message, features = call(
                between_kernel,
                (shaped((CHEADS, 3 * size, nodes), BF16), shaped((wide, nodes), F32)),
                [vmem()] * 4,
                (vmem(), vmem()),
                flops=2 * nodes * wide * 4 * wide,
                nbytes=nodes * wide * 8,
                name="between",
            )(back, features, out_turned[0], coarse_turned[1])
    return call(
        last_kernel,
        shaped((own, channels), F32),
        [smem()] + [vmem()] * 5,
        vmem(),
        [pltpu.VMEM((own, channels), F32)],
        flops=2 * nodes * wide * 3 * wide,
        nbytes=own * channels * 8,
        name="last",
    )(places, back, features, out_turned[1], unpool_weight, placed)


def solution(mesh):
    placed = (
        P(("leaf", "sub"), None),
        P(("leaf", "sub")),
        P(("leaf", "sub")),
        P("leaf", None),
        P(),
        P(),
        P(),
        P(),
        P(),
        P(),
    )
    return jax.shard_map(
        shards, mesh=mesh, in_specs=placed, out_specs=P(("leaf", "sub"), None), check_vma=False
    )
```

```python
import functools
import math

import jax
import jax.numpy as jnp
from jax import lax
from jax.experimental import pallas as pl
from jax.experimental.pallas import tpu as pltpu
from jax.sharding import PartitionSpec as P

HEADS = 4
CHEADS = 8
BALL = 256
GRAN = 32
LOG2E = 1.4426950408889634
NEG = -1e30
F32 = jnp.float32
BF16 = jnp.bfloat16


def vmem():
    return pl.BlockSpec(memory_space=pltpu.VMEM)


def smem():
    return pl.BlockSpec(memory_space=pltpu.SMEM)


def dot(a, b, dims=((1,), (0,))):
    return lax.dot_general(a, b, (dims, ((), ())), preferred_element_type=F32)


def call(kernel, out_shape, in_specs, out_specs, scratch=(), flops=0, nbytes=0, name=None, mib=16):
    return pl.pallas_call(
        kernel,
        out_shape=out_shape,
        in_specs=in_specs,
        out_specs=out_specs,
        scratch_shapes=list(scratch),
        cost_estimate=pl.CostEstimate(flops=flops, bytes_accessed=nbytes, transcendentals=0),
        compiler_params=pltpu.CompilerParams(vmem_limit_bytes=mib << 20),
        name=name,
    )


def ranks(classes, count):
    step = 256
    tri = (
        lax.broadcasted_iota(jnp.int32, (step, step), 0)
        <= lax.broadcasted_iota(jnp.int32, (step, step), 1)
    )
    tri = jnp.where(tri, 1.0, 0.0).astype(BF16)
    names = lax.broadcasted_iota(jnp.int32, (count, step), 0)
    carried = jnp.zeros((count, 1), F32)
    hots, found = [], []
    for row in classes:
        hot = jnp.where(names == row, 1.0, 0.0)
        hot16 = hot.astype(BF16)
        running = dot(hot16, tri) + carried
        found.append((jnp.sum(hot * running, axis=0, keepdims=True) - 1.0).astype(jnp.int32))
        hots.append(hot16)
        carried = running[:, step - 1 : step]
    return hots, found


def row_pairs(ref):
    return [
        jnp.concatenate([ref[2 * r : 2 * r + 1, :], ref[2 * r + 1 : 2 * r + 2, :]], axis=1)
        for r in range(ref.shape[0] // 2)
    ]


def store_pair(ref, r, value):
    ref[2 * r : 2 * r + 1, :] = value[:, :128]
    ref[2 * r + 1 : 2 * r + 2, :] = value[:, 128:]


def route_kernel(rot_ref, wanted_ref, slot_ref, *, own, devices):
    bucket = own // devices
    named = row_pairs(rot_ref)
    dest = [row // own for row in named]
    hots, found = ranks(dest, devices)
    lanes = lax.broadcasted_iota(jnp.int32, (bucket, 256), 0)
    total = jnp.zeros((devices, 2 * bucket), F32)
    for r, row in enumerate(named):
        store_pair(slot_ref, r, dest[r] * bucket + found[r])
        local = row % own
        here = lanes == found[r]
        high = jnp.where(here, (local // 64).astype(F32), 0.0)
        low = jnp.where(here, (local % 64).astype(F32), 0.0)
        parts = jnp.concatenate([high, low], axis=0).astype(BF16)
        total = total + dot(hots[r], parts, ((1,), (1,)))
    wanted = total[:, :bucket] * 64.0 + total[:, bucket:]
    wanted_ref[...] = jnp.zeros_like(wanted_ref)
    wanted_ref[:, :bucket] = wanted.astype(jnp.int32)


def place_kernel(pool_ref, place_ref, *, nodes):
    node = [row % nodes for row in row_pairs(pool_ref)]
    _, found = ranks(node, nodes)
    for r in range(len(node)):
        store_pair(place_ref, r, found[r] * nodes + node[r])


def norm_rows(x):
    centre = x - jnp.mean(x, axis=-1, keepdims=True)
    spread = jnp.mean(centre * centre, axis=-1, keepdims=True)
    return (centre * lax.rsqrt(spread + 1e-5)).astype(BF16)


def norm_columns(x):
    centre = x - jnp.mean(x, axis=0, keepdims=True)
    spread = jnp.mean(centre * centre, axis=0, keepdims=True)
    return (centre * lax.rsqrt(spread + 1e-5)).astype(BF16)


def ball(x, qkv_weight, out_weight):
    channels = x.shape[1]
    size = channels // HEADS
    normed = norm_rows(x)
    queries = dot(normed, qkv_weight[:, :channels]).astype(BF16)
    keys = dot(normed, qkv_weight[:, channels : 2 * channels]).astype(BF16)
    values = dot(normed, qkv_weight[:, 2 * channels :]).astype(BF16)
    values = jnp.concatenate([values, jnp.ones_like(values)], axis=1)
    head_of = lax.broadcasted_iota(jnp.int32, (1, channels), 1) // size
    summed = total = None
    for head in range(HEADS):
        mine = head_of == head
        scores = dot(jnp.where(mine, queries, jnp.zeros_like(queries)), keys, ((1,), (1,)))
        most = jnp.max(scores, axis=1, keepdims=True)
        weights = jnp.exp2((scores - most) * (LOG2E / math.sqrt(size))).astype(BF16)
        both = dot(weights, values)
        part, weight = both[:, :channels], both[:, channels:]
        summed = part if head == 0 else jnp.where(mine, part, summed)
        total = weight if head == 0 else jnp.where(mine, weight, total)
    return x + dot((summed / total).astype(BF16), out_weight)


def balls(x_ref, qkv_ref, out_ref, y_ref):
    together = 4

    def some(step, _):
        for j in range(together):
            rows = pl.ds(pl.multiple_of((step * together + j) * BALL, BALL), BALL)
            y_ref[rows, :] = ball(x_ref[rows, :], qkv_ref[...], out_ref[...])
        return 0

    lax.fori_loop(0, x_ref.shape[0] // (together * BALL), some, 0)


def first_kernel(x_ref, qkv_ref, out_ref, y_ref):
    balls(x_ref, qkv_ref.at[0], out_ref.at[0], y_ref)


def each_row(count, move):
    together = 64

    def some(step, _):
        for j in range(together):
            move(step * together + j)
        return 0

    lax.fori_loop(0, count // together, some, 0)


def each_slot(devices, bucket, move):
    together = 4

    def some(step, _):
        for i in range(together):
            for j in range(bucket):
                device = step * together + i
                move(device, j, device * bucket + j)
        return 0

    lax.fori_loop(0, devices // together, some, 0)


def answer_kernel(wanted_ref, x_ref, out_ref, rows_ref, *, bucket):
    def move(device, j, slot):
        rows_ref[pl.ds(slot, 1), :] = x_ref[pl.ds(wanted_ref[device, j], 1), :]

    each_slot(wanted_ref.shape[0], bucket, move)
    out_ref[...] = rows_ref[...].astype(BF16)


def second_kernel(slot_ref, x_ref, qkv_ref, out_ref, y_ref, slot_rows_ref, rows_ref):
    slot_rows_ref[...] = x_ref[...].astype(F32)

    def take(row):
        rows_ref[pl.ds(row, 1), :] = slot_rows_ref[pl.ds(slot_ref[row], 1), :]

    def give(row):
        slot_rows_ref[pl.ds(slot_ref[row], 1), :] = rows_ref[pl.ds(row, 1), :]

    each_row(rows_ref.shape[0], take)
    balls(rows_ref, qkv_ref.at[1], out_ref.at[1], rows_ref)
    each_row(rows_ref.shape[0], give)
    y_ref[...] = slot_rows_ref[...].astype(BF16)


def send_projected(features, weight_ref, layer, message_ref):
    normed = norm_columns(features)
    channels = features.shape[0]
    size = channels // CHEADS
    for part in range(3):
        projected = dot(weight_ref[layer, part * channels : (part + 1) * channels, :], normed).astype(BF16)
        for head in range(CHEADS):
            message_ref[head, part * size : (part + 1) * size, :] = projected[
                head * size : (head + 1) * size
            ]


def pool_kernel(
    wanted_ref, place_ref, x_ref, pool_ref, qkv_ref, message_ref, pooled_ref, placed_ref, from_ref, *, bucket
):
    from_ref[...] = x_ref[...].astype(F32)

    def move(device, j, slot):
        placed_ref[pl.ds(place_ref[wanted_ref[device, j]], 1), :] = from_ref[pl.ds(slot, 1), :]

    each_slot(wanted_ref.shape[0], bucket, move)
    nodes = x_ref.shape[0] // 8
    channels = x_ref.shape[1]
    pooled = None
    for k in range(8):
        part = dot(
            pool_ref[:, k * channels : (k + 1) * channels],
            placed_ref[k * nodes : (k + 1) * nodes, :].astype(BF16),
            ((1,), (1,)),
        )
        pooled = part if pooled is None else pooled + part
    pooled = pooled.astype(BF16).astype(F32)
    pooled_ref[...] = pooled
    send_projected(pooled, qkv_ref, 0, message_ref)


def coarse_kernel(counts_ref, x_ref, out_ref, keys_ref, values_ref, of_ref, first_ref, last_ref):
    tiles, parts, width = x_ref.shape
    size = parts // 3
    balls_here = counts_ref.shape[1]
    per_tile = width // GRAN
    together = 4
    scale = LOG2E / math.sqrt(size)
    for t in range(tiles):
        keys_ref[t] = x_ref[t, size : 2 * size, :].astype(F32).T.astype(BF16)
        values_ref[t] = jnp.concatenate([x_ref[t, 2 * size :, :], jnp.ones((16, width), BF16)], axis=0)
    start = 0
    ends = []
    for e in range(balls_here):
        end = start + counts_ref[0, e]

        def mark(block, _, e=e, start=start, end=end):
            of_ref[block] = e
            first_ref[block] = start
            last_ref[block] = end - 1
            return 0

        lax.fori_loop(start, end, mark, 0)
        ends.append(end)
        start = end

    def one(tile, _):
        queries = x_ref[tile, :size, :]
        blocks = tile * per_tile + lax.broadcasted_iota(jnp.int32, (1, width), 1) // GRAN
        own = jnp.zeros((1, width), jnp.int32)
        for e in range(balls_here):
            own = own + jnp.where(blocks >= ends[e], 1, 0)
        low = first_ref[tile * per_tile] // per_tile
        high = last_ref[tile * per_tile + per_tile - 1] // per_tile

        def add(step, carry):
            most, total = carry
            now = most
            chunks, chunk_scores = [], []
            for c in range(together):
                chunk = low + step * together + c
                live = chunk <= high
                chunk = jnp.minimum(chunk, high)
                scores = dot(keys_ref[chunk], queries)
                masked = []
                for g in range(per_tile):
                    ball_of = jnp.where(live, of_ref[chunk * per_tile + g], -1)
                    masked.append(jnp.where(own == ball_of, scores[g * GRAN : (g + 1) * GRAN], NEG))
                scores = jnp.concatenate(masked, axis=0)
                chunks.append(chunk)
                chunk_scores.append(scores)
                now = jnp.maximum(now, jnp.max(scores, axis=0, keepdims=True))
            total = total * jnp.exp2((most - now) * scale)
            for chunk, scores in zip(chunks, chunk_scores):
                weights = jnp.exp2((scores - now) * scale).astype(BF16)
                total = total + dot(values_ref[chunk], weights)
            return now, total

        begin = (jnp.full((1, width), NEG, F32), jnp.zeros((size + 16, width), F32))
        _, total = lax.fori_loop(0, (high - low + together) // together, add, begin)
        out_ref[tile] = (total[:size] / total[size : size + 1]).astype(BF16)
        return 0

    lax.fori_loop(0, tiles, one, 0)


def between_kernel(x_ref, features_ref, out_weight_ref, qkv_ref, message_ref, next_ref):
    heads, size, width = x_ref.shape
    features = features_ref[...] + dot(out_weight_ref[0], x_ref[...].reshape(heads * size, width))
    next_ref[...] = features
    send_projected(features, qkv_ref, 1, message_ref)


def last_kernel(place_ref, x_ref, features_ref, out_weight_ref, unpool_ref, placed_ref, out_ref, sum_ref):
    heads, size, width = x_ref.shape
    features = features_ref[...] + dot(out_weight_ref[1], x_ref[...].reshape(heads * size, width))
    features = features.astype(BF16).astype(F32)
    normed = norm_columns(features).astype(F32).T.astype(BF16)
    channels = placed_ref.shape[1]
    for k in range(8):
        rows = slice(k * width, (k + 1) * width)
        expanded = dot(normed, unpool_ref[:, k * channels : (k + 1) * channels])
        sum_ref[rows, :] = placed_ref[rows, :] + expanded

    def move(row):
        out_ref[pl.ds(row, 1), :] = sum_ref[pl.ds(place_ref[row], 1), :]

    each_row(out_ref.shape[0], move)


def shaped(shape, dtype):
    return jax.ShapeDtypeStruct(shape, dtype)


def exchange(value, axes):
    return lax.all_to_all(value, axes, split_axis=0, concat_axis=0, tiled=True)


def shards(
    beads,
    rot_perm,
    pool_ids,
    ball_counts,
    fine_qkv,
    fine_out,
    pool_weight,
    coarse_qkv,
    coarse_out,
    unpool_weight,
):
    own, channels = beads.shape
    both = ("leaf", "sub")
    subs = lax.axis_size("sub")
    devices = lax.axis_size("leaf") * subs
    bucket = own // devices
    nodes = own // 8
    wide = pool_weight.shape[1]
    size = wide // CHEADS
    wanted, slots = call(
        functools.partial(route_kernel, own=own, devices=devices),
        (shaped((devices, 128), jnp.int32), shaped((own // 128, 128), jnp.int32)),
        [vmem()],
        (vmem(), vmem()),
        flops=2 * devices * own * 256,
        nbytes=100000,
        name="route",
    )(rot_perm.reshape(own // 128, 128))
    requested = exchange(wanted.reshape(devices, 1, 128), both).reshape(devices, 128)
    places = call(
        functools.partial(place_kernel, nodes=nodes),
        shaped((own // 128, 128), jnp.int32),
        [vmem()],
        vmem(),
        flops=2 * nodes * own * 256,
        nbytes=20000,
        name="place",
    )(pool_ids.reshape(own // 128, 128))

    slots = slots.reshape(own)
    places = places.reshape(own)
    pool_turned = pool_weight.T
    coarse_turned = coarse_qkv.transpose(0, 2, 1)
    out_turned = coarse_out.transpose(0, 2, 1)
    ball_flops = own * channels * channels * 8 + own * BALL * channels * 16

    after_tree = call(
        first_kernel,
        shaped((own, channels), F32),
        [vmem()] * 3,
        vmem(),
        flops=ball_flops,
        nbytes=own * channels * 8,
        name="first",
    )(beads, fine_qkv, fine_out)
    answer = call(
        functools.partial(answer_kernel, bucket=bucket),
        shaped((own, channels), BF16),
        [smem(), vmem()],
        vmem(),
        [pltpu.VMEM((own, channels), F32)],
        nbytes=own * channels * 6,
        name="answer",
    )(requested, after_tree)
    arrived = exchange(answer.reshape(devices, bucket, channels), both).reshape(own, channels)
    outgoing = call(
        second_kernel,
        shaped((own, channels), BF16),
        [smem()] + [vmem()] * 3,
        vmem(),
        [pltpu.VMEM((own, channels), F32)] * 2,
        flops=ball_flops,
        nbytes=own * channels * 4,
        name="second",
    )(slots, arrived, fine_qkv, fine_out)
    coming = exchange(outgoing.reshape(devices, bucket, channels), both).reshape(own, channels)
    message, features, placed = call(
        functools.partial(pool_kernel, bucket=bucket),
        (
            shaped((CHEADS, 3 * size, nodes), BF16),
            shaped((wide, nodes), F32),
            shaped((own, channels), F32),
        ),
        [smem(), smem()] + [vmem()] * 3,
        (vmem(), vmem(), vmem()),
        [pltpu.VMEM((own, channels), F32)],
        flops=2 * nodes * wide * (own // 2 + 3 * wide),
        nbytes=own * channels * 8,
        name="pool",
    )(requested, places, coming, pool_turned, coarse_turned)
    for layer in range(2):
        received = exchange(message, "sub")
        attended = call(
            coarse_kernel,
            shaped((subs, size, nodes), BF16),
            [smem(), vmem()],
            vmem(),
            [pltpu.VMEM((subs, nodes, size), BF16), pltpu.VMEM((subs, size + 16, nodes), BF16)]
            + [pltpu.SMEM((subs * nodes // GRAN,), jnp.int32)] * 3,
            flops=subs * nodes * nodes * 3 * size * 4,
            nbytes=subs * nodes * size * 8,
            name="coarse",
        )(ball_counts, received)
        back = exchange(attended, "sub")
        if layer == 0:
            message, features = call(
                between_kernel,
                (shaped((CHEADS, 3 * size, nodes), BF16), shaped((wide, nodes), F32)),
                [vmem()] * 4,
                (vmem(), vmem()),
                flops=2 * nodes * wide * 4 * wide,
                nbytes=nodes * wide * 8,
                name="between",
            )(back, features, out_turned, coarse_turned)
    return call(
        last_kernel,
        shaped((own, channels), F32),
        [smem()] + [vmem()] * 5,
        vmem(),
        [pltpu.VMEM((own, channels), F32)],
        flops=2 * nodes * wide * 3 * wide,
        nbytes=own * channels * 8,
        name="last",
    )(places, back, features, out_turned, unpool_weight, placed)


def solution(mesh):
    placed = (
        P(("leaf", "sub"), None),
        P(("leaf", "sub")),
        P(("leaf", "sub")),
        P("leaf", None),
        P(),
        P(),
        P(),
        P(),
        P(),
        P(),
    )
    return jax.shard_map(
        shards, mesh=mesh, in_specs=placed, out_specs=P(("leaf", "sub"), None), check_vma=False
    )
```

```python
import functools
import math

import jax
import jax.numpy as jnp
from jax import lax
from jax.experimental import pallas as pl
from jax.experimental.pallas import tpu as pltpu
from jax.sharding import PartitionSpec as P

HEADS = 4
CHEADS = 8
BALL = 256
GRAN = 32
LOG2E = 1.4426950408889634
NEG = -1e30
F32 = jnp.float32
BF16 = jnp.bfloat16


def vmem():
    return pl.BlockSpec(memory_space=pltpu.VMEM)


def smem():
    return pl.BlockSpec(memory_space=pltpu.SMEM)


def hbm():
    return pl.BlockSpec(memory_space=pltpu.HBM)


def fetch(source, target, sem):
    copy = pltpu.make_async_copy(source, target, sem)
    copy.start()
    return copy


def dot(a, b, dims=((1,), (0,))):
    return lax.dot_general(a, b, (dims, ((), ())), preferred_element_type=F32)


def call(kernel, out_shape, in_specs, out_specs, scratch=(), flops=0, nbytes=0, name=None, mib=16):
    return pl.pallas_call(
        kernel,
        out_shape=out_shape,
        in_specs=in_specs,
        out_specs=out_specs,
        scratch_shapes=list(scratch),
        cost_estimate=pl.CostEstimate(flops=flops, bytes_accessed=nbytes, transcendentals=0),
        compiler_params=pltpu.CompilerParams(vmem_limit_bytes=mib << 20),
        name=name,
    )


def ranks(classes, count):
    step = 256
    tri = (
        lax.broadcasted_iota(jnp.int32, (step, step), 0)
        <= lax.broadcasted_iota(jnp.int32, (step, step), 1)
    )
    tri = jnp.where(tri, 1.0, 0.0).astype(BF16)
    names = lax.broadcasted_iota(jnp.int32, (count, step), 0)
    carried = jnp.zeros((count, 1), F32)
    hots, found = [], []
    for row in classes:
        hot = jnp.where(names == row, 1.0, 0.0)
        hot16 = hot.astype(BF16)
        running = dot(hot16, tri) + carried
        found.append((jnp.sum(hot * running, axis=0, keepdims=True) - 1.0).astype(jnp.int32))
        hots.append(hot16)
        carried = running[:, step - 1 : step]
    return hots, found


def row_pairs(ref):
    return [
        jnp.concatenate([ref[2 * r : 2 * r + 1, :], ref[2 * r + 1 : 2 * r + 2, :]], axis=1)
        for r in range(ref.shape[0] // 2)
    ]


def store_pair(ref, r, value):
    ref[2 * r : 2 * r + 1, :] = value[:, :128]
    ref[2 * r + 1 : 2 * r + 2, :] = value[:, 128:]


def route_kernel(rot_ref, wanted_ref, slot_ref, *, own, devices):
    bucket = own // devices
    named = row_pairs(rot_ref)
    dest = [row // own for row in named]
    hots, found = ranks(dest, devices)
    lanes = lax.broadcasted_iota(jnp.int32, (bucket, 256), 0)
    total = jnp.zeros((devices, 2 * bucket), F32)
    for r, row in enumerate(named):
        store_pair(slot_ref, r, dest[r] * bucket + found[r])
        local = row % own
        here = lanes == found[r]
        high = jnp.where(here, (local // 64).astype(F32), 0.0)
        low = jnp.where(here, (local % 64).astype(F32), 0.0)
        parts = jnp.concatenate([high, low], axis=0).astype(BF16)
        total = total + dot(hots[r], parts, ((1,), (1,)))
    wanted = total[:, :bucket] * 64.0 + total[:, bucket:]
    wanted_ref[...] = jnp.zeros_like(wanted_ref)
    wanted_ref[:, :bucket] = wanted.astype(jnp.int32)


def place_kernel(pool_ref, place_ref, *, nodes):
    node = [row % nodes for row in row_pairs(pool_ref)]
    _, found = ranks(node, nodes)
    for r in range(len(node)):
        store_pair(place_ref, r, found[r] * nodes + node[r])


def norm_rows(x):
    centre = x - jnp.mean(x, axis=-1, keepdims=True)
    spread = jnp.mean(centre * centre, axis=-1, keepdims=True)
    return (centre * lax.rsqrt(spread + 1e-5)).astype(BF16)


def norm_columns(x):
    centre = x - jnp.mean(x, axis=0, keepdims=True)
    spread = jnp.mean(centre * centre, axis=0, keepdims=True)
    return (centre * lax.rsqrt(spread + 1e-5)).astype(BF16)


def ball(x, qkv_weight, out_weight):
    channels = x.shape[1]
    size = channels // HEADS
    normed = norm_rows(x)
    queries = dot(normed, qkv_weight[:, :channels]).astype(BF16)
    keys = dot(normed, qkv_weight[:, channels : 2 * channels]).astype(BF16)
    values = dot(normed, qkv_weight[:, 2 * channels :]).astype(BF16)
    values = jnp.concatenate([values, jnp.ones_like(values)], axis=1)
    head_of = lax.broadcasted_iota(jnp.int32, (1, channels), 1) // size
    summed = total = None
    for head in range(HEADS):
        mine = head_of == head
        scores = dot(jnp.where(mine, queries, jnp.zeros_like(queries)), keys, ((1,), (1,)))
        most = jnp.max(scores, axis=1, keepdims=True)
        weights = jnp.exp2((scores - most) * (LOG2E / math.sqrt(size))).astype(BF16)
        both = dot(weights, values)
        part, weight = both[:, :channels], both[:, channels:]
        summed = part if head == 0 else jnp.where(mine, part, summed)
        total = weight if head == 0 else jnp.where(mine, weight, total)
    return x + dot((summed / total).astype(BF16), out_weight)


def first_kernel(x_ref, qkv_ref, out_ref, y_ref, held_ref, qkv_held, out_held, sems):
    rows = held_ref.shape[1]
    weights = [fetch(qkv_ref.at[0], qkv_held, sems.at[0]), fetch(out_ref.at[0], out_held, sems.at[1])]
    parts = [
        fetch(x_ref.at[pl.ds(p * rows, rows), :], held_ref.at[p], sems.at[2 + p])
        for p in range(held_ref.shape[0])
    ]
    for copy in weights:
        copy.wait()
    for p, copy in enumerate(parts):
        copy.wait()
        for j in range(rows // BALL):
            mine = slice(j * BALL, (j + 1) * BALL)
            at = p * rows + j * BALL
            y_ref[at : at + BALL, :] = ball(held_ref[p, mine, :], qkv_held[...], out_held[...])


def each_row(count, move):
    together = 64

    def some(step, _):
        for j in range(together):
            move(step * together + j)
        return 0

    lax.fori_loop(0, count // together, some, 0)


def answer_kernel(wanted_ref, x_ref, out_ref, named_ref, rows_ref, index_ref, sem, *, bucket):
    devices = wanted_ref.shape[0]
    per_row = 128 // bucket
    named_ref[...] = jnp.concatenate(
        [wanted_ref[pl.ds(i, devices // per_row, stride=per_row), :][:, :bucket] for i in range(per_row)],
        axis=1,
    )
    fetch(named_ref, index_ref, sem).wait()

    def some(step, _):
        for j in range(128):
            rows_ref[pl.ds(step * 128 + j, 1), :] = x_ref[pl.ds(index_ref[step, j], 1), :]
        return 0

    lax.fori_loop(0, index_ref.shape[0], some, 0)
    out_ref[...] = rows_ref[...].astype(BF16)


def second_kernel(slot_ref, x_ref, qkv_ref, out_ref, y_ref, from_ref, to_ref, in0, in1, out0, out1):
    ins, outs = (in0, in1), (out0, out1)
    count = x_ref.shape[0] // BALL
    from_ref[...] = x_ref[...].astype(F32)

    def take_first(row):
        in0[pl.ds(row, 1), :] = from_ref[pl.ds(slot_ref[row], 1), :]

    def give_last(row):
        slot = slot_ref[(count - 1) * BALL + row]
        to_ref[pl.ds(slot, 1), :] = outs[(count - 1) % 2][pl.ds(row, 1), :]

    each_row(BALL, take_first)
    for at in range(count):
        if at + 1 < count:
            for j in range(BALL):
                slot = slot_ref[(at + 1) * BALL + j]
                ins[(at + 1) % 2][j : j + 1, :] = from_ref[pl.ds(slot, 1), :]
        outs[at % 2][...] = ball(ins[at % 2][...], qkv_ref[1], out_ref[1])
        if at:
            for j in range(BALL):
                slot = slot_ref[(at - 1) * BALL + j]
                to_ref[pl.ds(slot, 1), :] = outs[(at - 1) % 2][j : j + 1, :]
    each_row(BALL, give_last)
    y_ref[...] = to_ref[...].astype(BF16)


def send_projected(features, weight_ref, message_ref):
    normed = norm_columns(features)
    channels = features.shape[0]
    size = channels // CHEADS
    for part in range(3):
        projected = dot(weight_ref[part * channels : (part + 1) * channels, :], normed).astype(BF16)
        for head in range(CHEADS):
            message_ref[head, part * size : (part + 1) * size, :] = projected[
                head * size : (head + 1) * size
            ]


def pool_kernel(
    named_ref,
    place_ref,
    x_ref,
    pool_ref,
    qkv_ref,
    message_ref,
    pooled_ref,
    placed_ref,
    from_ref,
    rows_ref,
    pool_held,
    qkv_held,
    pooled_held,
    sems,
):
    pool_copy = fetch(pool_ref, pool_held, sems.at[0])
    qkv_copy = fetch(qkv_ref.at[0], qkv_held, sems.at[1])
    from_ref[...] = x_ref[...].astype(F32)

    def move(slot):
        rows_ref[pl.ds(place_ref[named_ref[slot]], 1), :] = from_ref[pl.ds(slot, 1), :]

    each_row(from_ref.shape[0], move)
    placed_copy = fetch(rows_ref, placed_ref, sems.at[2])
    nodes = x_ref.shape[0] // 8
    channels = x_ref.shape[1]
    pool_copy.wait()
    pooled = None
    for k in range(8):
        part = dot(
            pool_held[:, k * channels : (k + 1) * channels],
            rows_ref[k * nodes : (k + 1) * nodes, :].astype(BF16),
            ((1,), (1,)),
        )
        pooled = part if pooled is None else pooled + part
    pooled = pooled.astype(BF16)
    pooled_held[...] = pooled
    pooled_copy = fetch(pooled_held, pooled_ref, sems.at[3])
    qkv_copy.wait()
    send_projected(pooled.astype(F32), qkv_held, message_ref)
    placed_copy.wait()
    pooled_copy.wait()


def coarse_kernel(counts_ref, x_ref, out_ref, keys_ref, values_ref, of_ref, first_ref, last_ref):
    tiles, parts, width = x_ref.shape
    size = parts // 3
    balls_here = counts_ref.shape[1]
    per_tile = width // GRAN
    together = 4
    scale = LOG2E / math.sqrt(size)
    for t in range(tiles):
        keys_ref[t] = x_ref[t, size : 2 * size, :].astype(F32).T.astype(BF16)
        values_ref[t] = jnp.concatenate([x_ref[t, 2 * size :, :], jnp.ones((16, width), BF16)], axis=0)
    start = 0
    ends = []
    for e in range(balls_here):
        end = start + counts_ref[0, e]

        def mark(block, _, e=e, start=start, end=end):
            of_ref[block] = e
            first_ref[block] = start
            last_ref[block] = end - 1
            return 0

        lax.fori_loop(start, end, mark, 0)
        ends.append(end)
        start = end

    def one(tile, _):
        queries = x_ref[tile, :size, :]
        blocks = tile * per_tile + lax.broadcasted_iota(jnp.int32, (1, width), 1) // GRAN
        own = jnp.zeros((1, width), jnp.int32)
        for e in range(balls_here):
            own = own + jnp.where(blocks >= ends[e], 1, 0)
        low = first_ref[tile * per_tile] // per_tile
        high = last_ref[tile * per_tile + per_tile - 1] // per_tile

        def add(step, carry):
            most, total = carry
            now = most
            chunks, chunk_scores = [], []
            for c in range(together):
                chunk = low + step * together + c
                live = chunk <= high
                chunk = jnp.minimum(chunk, high)
                scores = dot(keys_ref[chunk], queries)
                masked = []
                for g in range(per_tile):
                    ball_of = jnp.where(live, of_ref[chunk * per_tile + g], -1)
                    masked.append(jnp.where(own == ball_of, scores[g * GRAN : (g + 1) * GRAN], NEG))
                scores = jnp.concatenate(masked, axis=0)
                chunks.append(chunk)
                chunk_scores.append(scores)
                now = jnp.maximum(now, jnp.max(scores, axis=0, keepdims=True))
            total = total * jnp.exp2((most - now) * scale)
            for chunk, scores in zip(chunks, chunk_scores):
                weights = jnp.exp2((scores - now) * scale).astype(BF16)
                total = total + dot(values_ref[chunk], weights)
            return now, total

        begin = (jnp.full((1, width), NEG, F32), jnp.zeros((size + 16, width), F32))
        _, total = lax.fori_loop(0, (high - low + together) // together, add, begin)
        out_ref[tile] = (total[:size] / total[size : size + 1]).astype(BF16)
        return 0

    lax.fori_loop(0, tiles, one, 0)


def between_kernel(
    x_ref, features_ref, turned_ref, qkv_ref, message_ref, next_ref, features_held, out_held, qkv_held, next_held, sems
):
    out_copy = fetch(turned_ref.at[0], out_held, sems.at[0])
    features_copy = fetch(features_ref, features_held, sems.at[1])
    qkv_copy = fetch(qkv_ref.at[1], qkv_held, sems.at[2])
    heads, size, width = x_ref.shape
    out_copy.wait()
    added = dot(out_held[...], x_ref[...].reshape(heads * size, width))
    features_copy.wait()
    features = features_held[...].astype(F32) + added
    next_held[...] = features
    next_copy = fetch(next_held, next_ref, sems.at[3])
    qkv_copy.wait()
    send_projected(features, qkv_held, message_ref)
    next_copy.wait()


def last_kernel(
    place_ref,
    x_ref,
    features_ref,
    turned_ref,
    unpool_ref,
    placed_ref,
    out_ref,
    sum_ref,
    features_held,
    out_held,
    unpool_held,
    placed_held,
    sems,
):
    out_copy = fetch(turned_ref.at[1], out_held, sems.at[0])
    features_copy = fetch(features_ref, features_held, sems.at[1])
    unpool_copy = fetch(unpool_ref, unpool_held, sems.at[2])
    placed_copy = fetch(placed_ref, placed_held, sems.at[3])
    heads, size, width = x_ref.shape
    out_copy.wait()
    added = dot(out_held[...], x_ref[...].reshape(heads * size, width))
    features_copy.wait()
    features = (features_held[...] + added).astype(BF16).astype(F32)
    normed = norm_columns(features).astype(F32).T.astype(BF16)
    channels = placed_ref.shape[1]
    unpool_copy.wait()
    placed_copy.wait()
    for k in range(8):
        rows = slice(k * width, (k + 1) * width)
        expanded = dot(normed, unpool_held[:, k * channels : (k + 1) * channels])
        sum_ref[rows, :] = placed_held[rows, :] + expanded

    def move(row):
        out_ref[pl.ds(row, 1), :] = sum_ref[pl.ds(place_ref[row], 1), :]

    each_row(out_ref.shape[0], move)


def shaped(shape, dtype):
    return jax.ShapeDtypeStruct(shape, dtype)


def exchange(value, axes):
    return lax.all_to_all(value, axes, split_axis=0, concat_axis=0, tiled=True)


def shards(
    beads,
    rot_perm,
    pool_ids,
    ball_counts,
    fine_qkv,
    fine_out,
    pool_weight,
    coarse_qkv,
    coarse_out,
    unpool_weight,
):
    own, channels = beads.shape
    both = ("leaf", "sub")
    subs = lax.axis_size("sub")
    devices = lax.axis_size("leaf") * subs
    bucket = own // devices
    nodes = own // 8
    wide = pool_weight.shape[1]
    size = wide // CHEADS
    wanted, slots = call(
        functools.partial(route_kernel, own=own, devices=devices),
        (shaped((devices, 128), jnp.int32), shaped((own // 128, 128), jnp.int32)),
        [vmem()],
        (vmem(), vmem()),
        flops=2 * devices * own * 256,
        nbytes=100000,
        name="route",
    )(rot_perm.reshape(own // 128, 128))
    requested = exchange(wanted.reshape(devices, 1, 128), both).reshape(devices, 128)
    places = call(
        functools.partial(place_kernel, nodes=nodes),
        shaped((own // 128, 128), jnp.int32),
        [vmem()],
        vmem(),
        flops=2 * nodes * own * 256,
        nbytes=20000,
        name="place",
    )(pool_ids.reshape(own // 128, 128))

    slots = slots.reshape(own)
    places = places.reshape(own)
    ball_flops = own * channels * channels * 8 + own * BALL * channels * 16

    after_tree = call(
        first_kernel,
        shaped((own, channels), F32),
        [hbm()] * 3,
        vmem(),
        [
            pltpu.VMEM((2, own // 2, channels), F32),
            pltpu.VMEM((channels, 3 * channels), BF16),
            pltpu.VMEM((channels, channels), BF16),
            pltpu.SemaphoreType.DMA((4,)),
        ],
        flops=ball_flops,
        nbytes=own * channels * 8,
        name="first",
    )(beads, fine_qkv, fine_out)
    answer, named = call(
        functools.partial(answer_kernel, bucket=bucket),
        (shaped((own, channels), BF16), shaped((own // 128, 128), jnp.int32)),
        [vmem(), vmem()],
        (vmem(), vmem()),
        [
            pltpu.VMEM((own, channels), F32),
            pltpu.SMEM((own // 128, 128), jnp.int32),
            pltpu.SemaphoreType.DMA(()),
        ],
        nbytes=own * channels * 6,
        name="answer",
    )(requested, after_tree)
    named = named.reshape(own)
    arrived = exchange(answer.reshape(devices, bucket, channels), both).reshape(own, channels)
    outgoing = call(
        second_kernel,
        shaped((own, channels), BF16),
        [smem()] + [vmem()] * 3,
        vmem(),
        [pltpu.VMEM((own, channels), F32)] * 2 + [pltpu.VMEM((BALL, channels), F32)] * 4,
        flops=ball_flops,
        nbytes=own * channels * 4,
        name="second",
    )(slots, arrived, fine_qkv, fine_out)
    coming = exchange(outgoing.reshape(devices, bucket, channels), both).reshape(own, channels)
    pool_turned = pool_weight.T
    qkv_turned = coarse_qkv.transpose(0, 2, 1)
    out_turned = coarse_out.transpose(0, 2, 1)
    coming, pool_turned, qkv_turned, out_turned = lax.optimization_barrier(
        (coming, pool_turned, qkv_turned, out_turned)
    )
    message, features, placed = call(
        pool_kernel,
        (
            shaped((CHEADS, 3 * size, nodes), BF16),
            shaped((wide, nodes), BF16),
            shaped((own, channels), F32),
        ),
        [smem(), smem(), vmem(), hbm(), hbm()],
        (vmem(), hbm(), hbm()),
        [
            pltpu.VMEM((own, channels), F32),
            pltpu.VMEM((own, channels), F32),
            pltpu.VMEM((wide, own // 2), BF16),
            pltpu.VMEM((3 * wide, wide), BF16),
            pltpu.VMEM((wide, nodes), BF16),
            pltpu.SemaphoreType.DMA((4,)),
        ],
        flops=2 * nodes * wide * (own // 2 + 3 * wide),
        nbytes=own * channels * 8,
        name="pool",
    )(named, places, coming, pool_turned, qkv_turned)
    for layer in range(2):
        received = exchange(message, "sub")
        attended = call(
            coarse_kernel,
            shaped((subs, size, nodes), BF16),
            [smem(), vmem()],
            vmem(),
            [pltpu.VMEM((subs, nodes, size), BF16), pltpu.VMEM((subs, size + 16, nodes), BF16)]
            + [pltpu.SMEM((subs * nodes // GRAN,), jnp.int32)] * 3,
            flops=subs * nodes * nodes * 3 * size * 4,
            nbytes=subs * nodes * size * 8,
            name="coarse",
        )(ball_counts, received)
        back = exchange(attended, "sub")
        if layer == 0:
            message, features = call(
                between_kernel,
                (shaped((CHEADS, 3 * size, nodes), BF16), shaped((wide, nodes), F32)),
                [vmem(), hbm(), hbm(), hbm()],
                (vmem(), hbm()),
                [
                    pltpu.VMEM((wide, nodes), BF16),
                    pltpu.VMEM((wide, wide), BF16),
                    pltpu.VMEM((3 * wide, wide), BF16),
                    pltpu.VMEM((wide, nodes), F32),
                    pltpu.SemaphoreType.DMA((4,)),
                ],
                flops=2 * nodes * wide * 4 * wide,
                nbytes=nodes * wide * 8,
                name="between",
            )(back, features, out_turned, qkv_turned)
    return call(
        last_kernel,
        shaped((own, channels), F32),
        [smem(), vmem()] + [hbm()] * 4,
        vmem(),
        [
            pltpu.VMEM((own, channels), F32),
            pltpu.VMEM((wide, nodes), F32),
            pltpu.VMEM((wide, wide), BF16),
            pltpu.VMEM((wide, own // 2), BF16),
            pltpu.VMEM((own, channels), F32),
            pltpu.SemaphoreType.DMA((4,)),
        ],
        flops=2 * nodes * wide * 3 * wide,
        nbytes=own * channels * 8,
        name="last",
    )(places, back, features, out_turned, unpool_weight, placed)


def solution(mesh):
    placed = (
        P(("leaf", "sub"), None),
        P(("leaf", "sub")),
        P(("leaf", "sub")),
        P("leaf", None),
        P(),
        P(),
        P(),
        P(),
        P(),
        P(),
    )
    return jax.shard_map(
        shards, mesh=mesh, in_specs=placed, out_specs=P(("leaf", "sub"), None), check_vma=False
    )
```

```python
import functools
import math

import jax
import jax.numpy as jnp
from jax import lax
from jax.experimental import pallas as pl
from jax.experimental.pallas import tpu as pltpu
from jax.sharding import PartitionSpec as P

HEADS = 4
CHEADS = 8
BALL = 256
GRAN = 32
LOG2E = 1.4426950408889634
NEG = -1e30
F32 = jnp.float32
BF16 = jnp.bfloat16


def vmem():
    return pl.BlockSpec(memory_space=pltpu.VMEM)


def smem():
    return pl.BlockSpec(memory_space=pltpu.SMEM)


def hbm():
    return pl.BlockSpec(memory_space=pltpu.HBM)


def in_hbm(value):
    return pltpu.with_memory_space_constraint(value, pltpu.HBM)


def fetch(source, target, sem):
    copy = pltpu.make_async_copy(source, target, sem)
    copy.start()
    return copy


def dot(a, b, dims=((1,), (0,))):
    return lax.dot_general(a, b, (dims, ((), ())), preferred_element_type=F32)


def call(kernel, out_shape, in_specs, out_specs, scratch=(), flops=0, nbytes=0, name=None, mib=16):
    return pl.pallas_call(
        kernel,
        out_shape=out_shape,
        in_specs=in_specs,
        out_specs=out_specs,
        scratch_shapes=list(scratch),
        cost_estimate=pl.CostEstimate(flops=flops, bytes_accessed=nbytes, transcendentals=0),
        compiler_params=pltpu.CompilerParams(vmem_limit_bytes=mib << 20),
        name=name,
    )


def ranks(classes, count):
    step = 256
    tri = (
        lax.broadcasted_iota(jnp.int32, (step, step), 0)
        <= lax.broadcasted_iota(jnp.int32, (step, step), 1)
    )
    tri = jnp.where(tri, 1.0, 0.0).astype(BF16)
    names = lax.broadcasted_iota(jnp.int32, (count, step), 0)
    carried = jnp.zeros((count, 1), F32)
    hots, found = [], []
    for row in classes:
        hot = jnp.where(names == row, 1.0, 0.0)
        hot16 = hot.astype(BF16)
        running = dot(hot16, tri) + carried
        found.append((jnp.sum(hot * running, axis=0, keepdims=True) - 1.0).astype(jnp.int32))
        hots.append(hot16)
        carried = running[:, step - 1 : step]
    return hots, found


def row_pairs(ref):
    return [
        jnp.concatenate([ref[2 * r : 2 * r + 1, :], ref[2 * r + 1 : 2 * r + 2, :]], axis=1)
        for r in range(ref.shape[0] // 2)
    ]


def store_pair(ref, r, value):
    ref[2 * r : 2 * r + 1, :] = value[:, :128]
    ref[2 * r + 1 : 2 * r + 2, :] = value[:, 128:]


def route_kernel(rot_ref, wanted_ref, slot_ref, *, own, devices):
    bucket = own // devices
    named = row_pairs(rot_ref)
    dest = [row // own for row in named]
    hots, found = ranks(dest, devices)
    lanes = lax.broadcasted_iota(jnp.int32, (bucket, 256), 0)
    total = jnp.zeros((devices, 2 * bucket), F32)
    for r, row in enumerate(named):
        store_pair(slot_ref, r, dest[r] * bucket + found[r])
        local = row % own
        here = lanes == found[r]
        high = jnp.where(here, (local // 64).astype(F32), 0.0)
        low = jnp.where(here, (local % 64).astype(F32), 0.0)
        parts = jnp.concatenate([high, low], axis=0).astype(BF16)
        total = total + dot(hots[r], parts, ((1,), (1,)))
    wanted = total[:, :bucket] * 64.0 + total[:, bucket:]
    wanted_ref[...] = jnp.zeros_like(wanted_ref)
    wanted_ref[:, :bucket] = wanted.astype(jnp.int32)


def place_kernel(pool_ref, place_ref, *, nodes):
    node = [row % nodes for row in row_pairs(pool_ref)]
    _, found = ranks(node, nodes)
    for r in range(len(node)):
        store_pair(place_ref, r, found[r] * nodes + node[r])


def norm_rows(x):
    centre = x - jnp.mean(x, axis=-1, keepdims=True)
    spread = jnp.mean(centre * centre, axis=-1, keepdims=True)
    return (centre * lax.rsqrt(spread + 1e-5)).astype(BF16)


def norm_columns(x):
    centre = x - jnp.mean(x, axis=0, keepdims=True)
    spread = jnp.mean(centre * centre, axis=0, keepdims=True)
    return (centre * lax.rsqrt(spread + 1e-5)).astype(BF16)


def ball(x, qkv_weight, out_weight):
    channels = x.shape[1]
    size = channels // HEADS
    normed = norm_rows(x)
    queries = dot(normed, qkv_weight[:, :channels]).astype(BF16)
    keys = dot(normed, qkv_weight[:, channels : 2 * channels]).astype(BF16)
    values = dot(normed, qkv_weight[:, 2 * channels :]).astype(BF16)
    values = jnp.concatenate([values, jnp.ones_like(values)], axis=1)
    head_of = lax.broadcasted_iota(jnp.int32, (1, channels), 1) // size
    summed = total = None
    for head in range(HEADS):
        mine = head_of == head
        scores = dot(jnp.where(mine, queries, jnp.zeros_like(queries)), keys, ((1,), (1,)))
        most = jnp.max(scores, axis=1, keepdims=True)
        weights = jnp.exp2((scores - most) * (LOG2E / math.sqrt(size))).astype(BF16)
        both = dot(weights, values)
        part, weight = both[:, :channels], both[:, channels:]
        summed = part if head == 0 else jnp.where(mine, part, summed)
        total = weight if head == 0 else jnp.where(mine, weight, total)
    return x + dot((summed / total).astype(BF16), out_weight)


def first_kernel(x_ref, qkv_ref, out_ref, y_ref, held_ref, qkv_held, out_held, sems):
    rows = held_ref.shape[1]
    weights = [fetch(qkv_ref.at[0], qkv_held, sems.at[0]), fetch(out_ref.at[0], out_held, sems.at[1])]
    parts = [
        fetch(x_ref.at[pl.ds(p * rows, rows), :], held_ref.at[p], sems.at[2 + p])
        for p in range(held_ref.shape[0])
    ]
    for copy in weights:
        copy.wait()
    for p, copy in enumerate(parts):
        copy.wait()
        for j in range(rows // BALL):
            mine = slice(j * BALL, (j + 1) * BALL)
            at = p * rows + j * BALL
            y_ref[at : at + BALL, :] = ball(held_ref[p, mine, :], qkv_held[...], out_held[...])


def each_row(count, move):
    together = 64

    def some(step, _):
        for j in range(together):
            move(step * together + j)
        return 0

    lax.fori_loop(0, count // together, some, 0)


def answer_kernel(wanted_ref, x_ref, out_ref, named_ref, rows_ref, index_ref, sem, *, bucket):
    devices = wanted_ref.shape[0]
    per_row = 128 // bucket
    named_ref[...] = jnp.concatenate(
        [wanted_ref[pl.ds(i, devices // per_row, stride=per_row), :][:, :bucket] for i in range(per_row)],
        axis=1,
    )
    fetch(named_ref, index_ref, sem).wait()

    def some(step, _):
        for j in range(128):
            rows_ref[pl.ds(step * 128 + j, 1), :] = x_ref[pl.ds(index_ref[step, j], 1), :]
        return 0

    lax.fori_loop(0, index_ref.shape[0], some, 0)
    out_ref[...] = rows_ref[...].astype(BF16)


def second_kernel(slot_ref, x_ref, qkv_ref, out_ref, y_ref, from_ref, to_ref, in0, in1, out0, out1):
    ins, outs = (in0, in1), (out0, out1)
    count = x_ref.shape[0] // BALL
    from_ref[...] = x_ref[...].astype(F32)

    def take_first(row):
        in0[pl.ds(row, 1), :] = from_ref[pl.ds(slot_ref[row], 1), :]

    def give_last(row):
        slot = slot_ref[(count - 1) * BALL + row]
        to_ref[pl.ds(slot, 1), :] = outs[(count - 1) % 2][pl.ds(row, 1), :]

    each_row(BALL, take_first)
    for at in range(count):
        if at + 1 < count:
            for j in range(BALL):
                slot = slot_ref[(at + 1) * BALL + j]
                ins[(at + 1) % 2][j : j + 1, :] = from_ref[pl.ds(slot, 1), :]
        outs[at % 2][...] = ball(ins[at % 2][...], qkv_ref[1], out_ref[1])
        if at:
            for j in range(BALL):
                slot = slot_ref[(at - 1) * BALL + j]
                to_ref[pl.ds(slot, 1), :] = outs[(at - 1) % 2][j : j + 1, :]
    each_row(BALL, give_last)
    y_ref[...] = to_ref[...].astype(BF16)


def send_projected(features, weight, message_ref):
    normed = norm_columns(features)
    channels = features.shape[0]
    size = channels // CHEADS
    for part in range(3):
        projected = dot(weight[part * channels : (part + 1) * channels, :], normed).astype(BF16)
        for head in range(CHEADS):
            message_ref[head, part * size : (part + 1) * size, :] = projected[
                head * size : (head + 1) * size
            ]


def pool_kernel(
    named_ref, place_ref, x_ref, pool_ref, qkv_ref, message_ref, pooled_ref, placed_ref, from_ref, held_ref, sem
):
    weight_copy = fetch(pool_ref, held_ref, sem)
    from_ref[...] = x_ref[...].astype(F32)

    def move(slot):
        placed_ref[pl.ds(place_ref[named_ref[slot]], 1), :] = from_ref[pl.ds(slot, 1), :]

    each_row(from_ref.shape[0], move)
    nodes = x_ref.shape[0] // 8
    channels = x_ref.shape[1]
    weight_copy.wait()
    pooled = None
    for k in range(8):
        part = dot(
            placed_ref[k * nodes : (k + 1) * nodes, :].astype(BF16),
            held_ref[k * channels : (k + 1) * channels, :],
        )
        pooled = part if pooled is None else pooled + part
    pooled = pooled.astype(BF16).astype(F32).T
    pooled_ref[...] = pooled
    send_projected(pooled, qkv_ref[0], message_ref)


def coarse_kernel(counts_ref, x_ref, out_ref, keys_ref, values_ref, of_ref, first_ref, last_ref, most_ref, total_ref):
    tiles, parts, width = x_ref.shape
    size = parts // 3
    balls_here = counts_ref.shape[1]
    per_tile = width // GRAN
    top = 4
    scale = LOG2E / math.sqrt(size)
    for t in range(tiles):
        keys_ref[t] = x_ref[t, size : 2 * size, :].astype(F32).T.astype(BF16)
        values_ref[t] = jnp.concatenate([x_ref[t, 2 * size :, :], jnp.ones((16, width), BF16)], axis=0)
    start = 0
    ends = []
    for e in range(balls_here):
        end = start + counts_ref[0, e]
        def mark(block, _, e=e, start=start, end=end):
            of_ref[block] = e
            first_ref[block] = start
            last_ref[block] = end - 1
            return 0
        lax.fori_loop(start, end, mark, 0)
        ends.append(end)
        start = end

    def one(tile, _):
        queries = x_ref[tile, :size, :]
        blocks = tile * per_tile + lax.broadcasted_iota(jnp.int32, (1, width), 1) // GRAN
        own = jnp.zeros((1, width), jnp.int32)
        for e in range(balls_here):
            own = own + jnp.where(blocks >= ends[e], 1, 0)
        low = first_ref[tile * per_tile] // per_tile
        high = last_ref[tile * per_tile + per_tile - 1] // per_tile

        def scored(chunk):
            scores = dot(keys_ref[chunk], queries)
            return jnp.concatenate(
                [
                    jnp.where(own == of_ref[chunk * per_tile + g], scores[g * GRAN : (g + 1) * GRAN], NEG)
                    for g in range(per_tile)
                ],
                axis=0,
            )

        def several(chunk, count, carried):
            scores = [scored(chunk + c) for c in range(count)]
            now = most = most_ref[...] if carried else None
            for s in scores:
                here = jnp.max(s, axis=0, keepdims=True)
                now = here if now is None else jnp.maximum(now, here)
            total = total_ref[...] * jnp.exp2((most - now) * scale) if carried else None
            for c, s in enumerate(scores):
                part = dot(values_ref[chunk + c], jnp.exp2((s - now) * scale).astype(BF16))
                total = part if total is None else total + part
            most_ref[...] = now
            total_ref[...] = total

        number = high - low + 1
        head = jnp.where(number <= top, number, jnp.where(number == top + 1, top - 1, top))
        for count in range(1, top + 1):
            @pl.when(head == count)
            def _(count=count):
                several(low, count, False)
        def more(step, _):
            chunk = low + head + step * 2
            left = high - chunk + 1
            @pl.when(left >= 2)
            def _(): several(chunk, 2, True)
            @pl.when(left == 1)
            def _(): several(chunk, 1, True)
            return 0
        lax.fori_loop(0, (number - head + 1) // 2, more, 0)
        total = total_ref[...]
        out_ref[tile] = (total[:size] / total[size : size + 1]).astype(BF16)
        return 0

    lax.fori_loop(0, tiles, one, 0)


def between_kernel(x_ref, features_ref, turned_ref, qkv_ref, message_ref, next_ref):
    heads, size, width = x_ref.shape
    features = features_ref[...] + dot(turned_ref[0], x_ref[...].reshape(heads * size, width))
    next_ref[...] = features
    send_projected(features, qkv_ref[1], message_ref)


def last_kernel(
    place_ref, x_ref, features_ref, turned_ref, unpool_ref, placed_ref, out_ref, sum_ref, rows_ref, sems
):
    heads, size, width = x_ref.shape
    features = features_ref[...] + dot(turned_ref[1], x_ref[...].reshape(heads * size, width))
    features = features.astype(BF16).astype(F32)
    normed = norm_columns(features).astype(F32).T.astype(BF16)
    channels = placed_ref.shape[1]
    for k in range(8):
        rows = slice(k * width, (k + 1) * width)
        expanded = dot(normed, unpool_ref[:, k * channels : (k + 1) * channels])
        sum_ref[rows, :] = placed_ref[rows, :] + expanded
    parts = sems.shape[0]
    count = rows_ref.shape[0] // parts
    copies = []
    for p in range(parts):

        def move(row, p=p):
            at = p * count + row
            rows_ref[pl.ds(at, 1), :] = sum_ref[pl.ds(place_ref[at], 1), :]

        each_row(count, move)
        mine = pl.ds(p * count, count)
        copies.append(fetch(rows_ref.at[mine, :], out_ref.at[mine, :], sems.at[p]))
    for copy in copies:
        copy.wait()


def shaped(shape, dtype):
    return jax.ShapeDtypeStruct(shape, dtype)


def exchange(value, axes):
    return lax.all_to_all(value, axes, split_axis=0, concat_axis=0, tiled=True)


def shards(
    beads,
    rot_perm,
    pool_ids,
    ball_counts,
    fine_qkv,
    fine_out,
    pool_weight,
    coarse_qkv,
    coarse_out,
    unpool_weight,
):
    own, channels = beads.shape
    both = ("leaf", "sub")
    subs = lax.axis_size("sub")
    devices = lax.axis_size("leaf") * subs
    bucket = own // devices
    nodes = own // 8
    wide = pool_weight.shape[1]
    size = wide // CHEADS
    wanted, slots = call(
        functools.partial(route_kernel, own=own, devices=devices),
        (shaped((devices, 128), jnp.int32), shaped((own // 128, 128), jnp.int32)),
        [vmem()],
        (vmem(), vmem()),
        flops=2 * devices * own * 256,
        nbytes=100000,
        name="route",
    )(rot_perm.reshape(own // 128, 128))
    requested = exchange(wanted.reshape(devices, 1, 128), both).reshape(devices, 128)
    places = call(
        functools.partial(place_kernel, nodes=nodes),
        shaped((own // 128, 128), jnp.int32),
        [vmem()],
        vmem(),
        flops=2 * nodes * own * 256,
        nbytes=20000,
        name="place",
    )(pool_ids.reshape(own // 128, 128))

    slots = slots.reshape(own)
    places = places.reshape(own)
    ball_flops = own * channels * channels * 8 + own * BALL * channels * 16

    after_tree = call(
        first_kernel,
        shaped((own, channels), F32),
        [hbm()] * 3,
        vmem(),
        [
            pltpu.VMEM((2, own // 2, channels), F32),
            pltpu.VMEM((channels, 3 * channels), BF16),
            pltpu.VMEM((channels, channels), BF16),
            pltpu.SemaphoreType.DMA((4,)),
        ],
        flops=ball_flops,
        nbytes=own * channels * 8,
        name="first",
    )(in_hbm(beads), in_hbm(fine_qkv), in_hbm(fine_out))
    answer, named = call(
        functools.partial(answer_kernel, bucket=bucket),
        (shaped((own, channels), BF16), shaped((own // 128, 128), jnp.int32)),
        [vmem(), vmem()],
        (vmem(), vmem()),
        [
            pltpu.VMEM((own, channels), F32),
            pltpu.SMEM((own // 128, 128), jnp.int32),
            pltpu.SemaphoreType.DMA(()),
        ],
        nbytes=own * channels * 6,
        name="answer",
    )(requested, after_tree)
    named = named.reshape(own)
    arrived = exchange(answer.reshape(devices, bucket, channels), both).reshape(own, channels)
    outgoing = call(
        second_kernel,
        shaped((own, channels), BF16),
        [smem()] + [vmem()] * 3,
        vmem(),
        [pltpu.VMEM((own, channels), F32)] * 2 + [pltpu.VMEM((BALL, channels), F32)] * 4,
        flops=ball_flops,
        nbytes=own * channels * 4,
        name="second",
    )(slots, arrived, fine_qkv, fine_out)
    coming = exchange(outgoing.reshape(devices, bucket, channels), both).reshape(own, channels)
    qkv_turned = coarse_qkv.transpose(0, 2, 1)
    out_turned = coarse_out.transpose(0, 2, 1)
    coming, qkv_turned, out_turned = lax.optimization_barrier((coming, qkv_turned, out_turned))
    message, features, placed = call(
        pool_kernel,
        (
            shaped((CHEADS, 3 * size, nodes), BF16),
            shaped((wide, nodes), F32),
            shaped((own, channels), F32),
        ),
        [smem(), smem(), vmem(), hbm(), vmem()],
        (vmem(), vmem(), vmem()),
        [
            pltpu.VMEM((own, channels), F32),
            pltpu.VMEM((own // 2, wide), BF16),
            pltpu.SemaphoreType.DMA(()),
        ],
        flops=2 * nodes * wide * (own // 2 + 3 * wide),
        nbytes=own * channels * 8,
        name="pool",
    )(named, places, coming, in_hbm(pool_weight), qkv_turned)
    for layer in range(2):
        received = exchange(message, "sub")
        attended = call(
            coarse_kernel,
            shaped((subs, size, nodes), BF16),
            [smem(), vmem()],
            vmem(),
            [pltpu.VMEM((subs, nodes, size), BF16), pltpu.VMEM((subs, size + 16, nodes), BF16)]
            + [pltpu.SMEM((subs * nodes // GRAN,), jnp.int32)] * 3
            + [pltpu.VMEM((1, nodes), F32), pltpu.VMEM((size + 16, nodes), F32)],
            flops=subs * nodes * nodes * 3 * size * 4,
            nbytes=subs * nodes * size * 8,
            name="coarse",
        )(ball_counts, received)
        back = exchange(attended, "sub")
        if layer == 0:
            message, features = call(
                between_kernel,
                (shaped((CHEADS, 3 * size, nodes), BF16), shaped((wide, nodes), F32)),
                [vmem()] * 4,
                (vmem(), vmem()),
                flops=2 * nodes * wide * 4 * wide,
                nbytes=nodes * wide * 8,
                name="between",
            )(back, features, out_turned, qkv_turned)
    return call(
        last_kernel,
        shaped((own, channels), F32),
        [smem()] + [vmem()] * 5,
        hbm(),
        [
            pltpu.VMEM((own, channels), F32),
            pltpu.VMEM((own, channels), F32),
            pltpu.SemaphoreType.DMA((4,)),
        ],
        flops=2 * nodes * wide * 3 * wide,
        nbytes=own * channels * 8,
        name="last",
    )(places, back, features, out_turned, unpool_weight, placed)


def solution(mesh):
    placed = (
        P(("leaf", "sub"), None),
        P(("leaf", "sub")),
        P(("leaf", "sub")),
        P("leaf", None),
        P(),
        P(),
        P(),
        P(),
        P(),
        P(),
    )
    return jax.shard_map(
        shards, mesh=mesh, in_specs=placed, out_specs=P(("leaf", "sub"), None), check_vma=False
    )
```

```python
import functools
import math

import jax
import jax.numpy as jnp
from jax import lax
from jax.experimental import pallas as pl
from jax.experimental.pallas import tpu as pltpu
from jax.sharding import PartitionSpec as P

HEADS = 4
CHEADS = 8
BALL = 256
GRAN = 32
LOG2E = 1.4426950408889634
NEG = -1e30
F32 = jnp.float32
BF16 = jnp.bfloat16


def vmem():
    return pl.BlockSpec(memory_space=pltpu.VMEM)


def smem():
    return pl.BlockSpec(memory_space=pltpu.SMEM)


def hbm():
    return pl.BlockSpec(memory_space=pltpu.HBM)


def in_hbm(value):
    return pltpu.with_memory_space_constraint(value, pltpu.HBM)


def fetch(source, target, sem):
    copy = pltpu.make_async_copy(source, target, sem)
    copy.start()
    return copy


def dot(a, b, dims=((1,), (0,))):
    return lax.dot_general(a, b, (dims, ((), ())), preferred_element_type=F32)


def call(kernel, out_shape, in_specs, out_specs, scratch=(), flops=0, nbytes=0, name=None, mib=16):
    return pl.pallas_call(
        kernel,
        out_shape=out_shape,
        in_specs=in_specs,
        out_specs=out_specs,
        scratch_shapes=list(scratch),
        cost_estimate=pl.CostEstimate(flops=flops, bytes_accessed=nbytes, transcendentals=0),
        compiler_params=pltpu.CompilerParams(vmem_limit_bytes=mib << 20),
        name=name,
    )


def ranks(classes, count):
    step = 256
    tri = (
        lax.broadcasted_iota(jnp.int32, (step, step), 0)
        <= lax.broadcasted_iota(jnp.int32, (step, step), 1)
    )
    tri = jnp.where(tri, 1.0, 0.0).astype(BF16)
    names = lax.broadcasted_iota(jnp.int32, (count, step), 0)
    carried = jnp.zeros((count, 1), F32)
    hots, found = [], []
    for row in classes:
        hot = jnp.where(names == row, 1.0, 0.0)
        hot16 = hot.astype(BF16)
        running = dot(hot16, tri) + carried
        found.append((jnp.sum(hot * running, axis=0, keepdims=True) - 1.0).astype(jnp.int32))
        hots.append(hot16)
        carried = running[:, step - 1 : step]
    return hots, found


def row_pairs(ref):
    return [
        jnp.concatenate([ref[2 * r : 2 * r + 1, :], ref[2 * r + 1 : 2 * r + 2, :]], axis=1)
        for r in range(ref.shape[0] // 2)
    ]


def store_pair(ref, r, value):
    ref[2 * r : 2 * r + 1, :] = value[:, :128]
    ref[2 * r + 1 : 2 * r + 2, :] = value[:, 128:]


def route_kernel(rot_ref, wanted_ref, slot_ref, *, own, devices):
    bucket = own // devices
    named = row_pairs(rot_ref)
    own_bits = own.bit_length() - 1
    dest = [row >> own_bits for row in named]
    hots, found = ranks(dest, devices)
    lanes = lax.broadcasted_iota(jnp.int32, (bucket, 256), 0)
    total = jnp.zeros((devices, 2 * bucket), F32)
    for r, row in enumerate(named):
        store_pair(slot_ref, r, dest[r] * bucket + found[r])
        local = row & (own - 1)
        here = lanes == found[r]
        high = jnp.where(here, (local >> 6).astype(F32), 0.0)
        low = jnp.where(here, (local & 63).astype(F32), 0.0)
        parts = jnp.concatenate([high, low], axis=0).astype(BF16)
        total = total + dot(hots[r], parts, ((1,), (1,)))
    wanted = total[:, :bucket] * 64.0 + total[:, bucket:]
    wanted_ref[...] = jnp.zeros_like(wanted_ref)
    wanted_ref[:, :bucket] = wanted.astype(jnp.int32)


def place_kernel(pool_ref, place_ref, *, nodes):
    node = [row & (nodes - 1) for row in row_pairs(pool_ref)]
    _, found = ranks(node, nodes)
    for r in range(len(node)):
        store_pair(place_ref, r, found[r] * nodes + node[r])


def norm_rows(x):
    centre = x - jnp.mean(x, axis=-1, keepdims=True)
    spread = jnp.mean(centre * centre, axis=-1, keepdims=True)
    return (centre * lax.rsqrt(spread + 1e-5)).astype(BF16)


def norm_columns(x):
    centre = x - jnp.mean(x, axis=0, keepdims=True)
    spread = jnp.mean(centre * centre, axis=0, keepdims=True)
    return (centre * lax.rsqrt(spread + 1e-5)).astype(BF16)


def ball(x, qkv_weight, out_weight):
    channels = x.shape[1]
    size = channels // HEADS
    normed = norm_rows(x)
    queries = dot(normed, qkv_weight[:, :channels]).astype(BF16)
    keys = dot(normed, qkv_weight[:, channels : 2 * channels]).astype(BF16)
    values = dot(normed, qkv_weight[:, 2 * channels :]).astype(BF16)
    values = jnp.concatenate([values, jnp.ones_like(values)], axis=1)
    head_of = lax.broadcasted_iota(jnp.int32, (1, channels), 1) // size
    summed = total = None
    for head in range(HEADS):
        mine = head_of == head
        scores = dot(jnp.where(mine, queries, jnp.zeros_like(queries)), keys, ((1,), (1,)))
        most = jnp.max(scores, axis=1, keepdims=True)
        weights = jnp.exp2((scores - most) * (LOG2E / math.sqrt(size))).astype(BF16)
        both = dot(weights, values)
        part, weight = both[:, :channels], both[:, channels:]
        summed = part if head == 0 else jnp.where(mine, part, summed)
        total = weight if head == 0 else jnp.where(mine, weight, total)
    return x + dot((summed / total).astype(BF16), out_weight)


def first_kernel(x_ref, qkv_ref, out_ref, y_ref, held_ref, qkv_held, out_held, sems):
    rows = held_ref.shape[1]
    weights = [fetch(qkv_ref.at[0], qkv_held, sems.at[0]), fetch(out_ref.at[0], out_held, sems.at[1])]
    parts = [
        fetch(x_ref.at[pl.ds(p * rows, rows), :], held_ref.at[p], sems.at[2 + p])
        for p in range(held_ref.shape[0])
    ]
    for copy in weights:
        copy.wait()
    for p, copy in enumerate(parts):
        copy.wait()
        for j in range(rows // BALL):
            mine = slice(j * BALL, (j + 1) * BALL)
            at = p * rows + j * BALL
            y_ref[at : at + BALL, :] = ball(held_ref[p, mine, :], qkv_held[...], out_held[...])


def each_row(count, move):
    together = 64

    def some(step, _):
        for j in range(together):
            move(step * together + j)
        return 0

    lax.fori_loop(0, count // together, some, 0)


def answer_kernel(wanted_ref, x_ref, out_ref, named_ref, rows_ref, index_ref, sem, *, bucket):
    devices = wanted_ref.shape[0]
    per_row = 128 // bucket
    named_ref[...] = jnp.concatenate(
        [wanted_ref[pl.ds(i, devices // per_row, stride=per_row), :][:, :bucket] for i in range(per_row)],
        axis=1,
    )
    fetch(named_ref, index_ref, sem).wait()

    def some(step, _):
        for j in range(128):
            rows_ref[pl.ds(step * 128 + j, 1), :] = x_ref[pl.ds(index_ref[step, j], 1), :]
        return 0

    lax.fori_loop(0, index_ref.shape[0], some, 0)
    out_ref[...] = rows_ref[...].astype(BF16)


def second_kernel(slot_ref, x_ref, qkv_ref, out_ref, y_ref, from_ref, to_ref, in0, in1, out0, out1):
    ins, outs = (in0, in1), (out0, out1)
    count = x_ref.shape[0] // BALL
    from_ref[...] = x_ref[...].astype(F32)

    def take_first(row):
        in0[pl.ds(row, 1), :] = from_ref[pl.ds(slot_ref[row], 1), :]

    def give_last(row):
        slot = slot_ref[(count - 1) * BALL + row]
        to_ref[pl.ds(slot, 1), :] = outs[(count - 1) % 2][pl.ds(row, 1), :]

    each_row(BALL, take_first)
    for at in range(count):
        if at + 1 < count:
            for j in range(BALL):
                slot = slot_ref[(at + 1) * BALL + j]
                ins[(at + 1) % 2][j : j + 1, :] = from_ref[pl.ds(slot, 1), :]
        outs[at % 2][...] = ball(ins[at % 2][...], qkv_ref[1], out_ref[1])
        if at:
            for j in range(BALL):
                slot = slot_ref[(at - 1) * BALL + j]
                to_ref[pl.ds(slot, 1), :] = outs[(at - 1) % 2][j : j + 1, :]
    each_row(BALL, give_last)
    y_ref[...] = to_ref[...].astype(BF16)


def send_projected(features, weight, message_ref):
    normed = norm_columns(features)
    channels = features.shape[0]
    size = channels // CHEADS
    for part in range(3):
        projected = dot(weight[part * channels : (part + 1) * channels, :], normed).astype(BF16)
        for head in range(CHEADS):
            message_ref[head, part * size : (part + 1) * size, :] = projected[
                head * size : (head + 1) * size
            ]


def pool_kernel(
    named_ref, place_ref, x_ref, pool_ref, qkv_ref, message_ref, pooled_ref, placed_ref, from_ref, held_ref, sem
):
    weight_copy = fetch(pool_ref, held_ref, sem)
    from_ref[...] = x_ref[...].astype(F32)

    def move(slot):
        placed_ref[pl.ds(place_ref[named_ref[slot]], 1), :] = from_ref[pl.ds(slot, 1), :]

    each_row(from_ref.shape[0], move)
    nodes = x_ref.shape[0] // 8
    channels = x_ref.shape[1]
    weight_copy.wait()
    pooled = None
    for k in range(8):
        part = dot(
            placed_ref[k * nodes : (k + 1) * nodes, :].astype(BF16),
            held_ref[k * channels : (k + 1) * channels, :],
        )
        pooled = part if pooled is None else pooled + part
    pooled = pooled.astype(BF16).astype(F32).T
    pooled_ref[...] = pooled
    send_projected(pooled, qkv_ref[0], message_ref)


def coarse_kernel(counts_ref, x_ref, out_ref, keys_ref, values_ref, most_ref, total_ref):
    tiles, parts, width = x_ref.shape
    size = parts // 3
    per_tile = width // GRAN
    top = 4
    scale = LOG2E / math.sqrt(size)
    for t in range(tiles):
        keys_ref[t] = x_ref[t, size : 2 * size, :].astype(F32).T.astype(BF16)
        values_ref[t] = jnp.concatenate([x_ref[t, 2 * size :, :], jnp.ones((16, width), BF16)], axis=0)
    edges = [counts_ref[0, 0]]
    for e in range(1, counts_ref.shape[1] - 1):
        edges.append(edges[-1] + counts_ref[0, e])
    lane_block = lax.broadcasted_iota(jnp.int32, (1, width), 1) >> (GRAN.bit_length() - 1)
    tile_bits = per_tile.bit_length() - 1

    def ball_around(block):
        begin, end = 0, tiles * per_tile
        for edge in edges:
            begin = jnp.where(edge <= block, edge, begin)
        for edge in reversed(edges):
            end = jnp.where(edge > block, edge, end)
        return begin, end

    def one(tile, _):
        queries = x_ref[tile, :size, :]
        begin, end = ball_around(tile * per_tile + lane_block)
        low = ball_around(tile * per_tile)[0] >> tile_bits
        high = (ball_around(tile * per_tile + per_tile - 1)[1] - 1) >> tile_bits

        def scored(chunk):
            scores = dot(keys_ref[chunk], queries)
            masked = []
            for g in range(per_tile):
                block = chunk * per_tile + g
                seen = jnp.logical_and(block >= begin, block < end)
                masked.append(jnp.where(seen, scores[g * GRAN : (g + 1) * GRAN], NEG))
            return jnp.concatenate(masked, axis=0)

        def several(chunk, count, carried):
            scores = [scored(chunk + c) for c in range(count)]
            now = most = most_ref[...] if carried else None
            for s in scores:
                here = jnp.max(s, axis=0, keepdims=True)
                now = here if now is None else jnp.maximum(now, here)
            total = total_ref[...] * jnp.exp2((most - now) * scale) if carried else None
            for c, s in enumerate(scores):
                part = dot(values_ref[chunk + c], jnp.exp2((s - now) * scale).astype(BF16))
                total = part if total is None else total + part
            most_ref[...] = now
            total_ref[...] = total

        number = high - low + 1
        head = jnp.where(number <= top, number, jnp.where(number == top + 1, top - 1, top))
        for count in range(1, top + 1):

            @pl.when(head == count)
            def _(count=count):
                several(low, count, False)

        def more(step, _):
            chunk = low + head + step * 2
            left = high - chunk + 1

            @pl.when(left >= 2)
            def _():
                several(chunk, 2, True)

            @pl.when(left == 1)
            def _():
                several(chunk, 1, True)

            return 0

        lax.fori_loop(0, (number - head + 1) >> 1, more, 0)
        total = total_ref[...]
        out_ref[tile] = (total[:size] / total[size : size + 1]).astype(BF16)
        return 0

    lax.fori_loop(0, tiles, one, 0)


def between_kernel(x_ref, features_ref, turned_ref, qkv_ref, message_ref, next_ref):
    heads, size, width = x_ref.shape
    features = features_ref[...] + dot(turned_ref[0], x_ref[...].reshape(heads * size, width))
    next_ref[...] = features
    send_projected(features, qkv_ref[1], message_ref)


def last_kernel(
    place_ref, x_ref, features_ref, turned_ref, unpool_ref, placed_ref, out_ref, sum_ref, rows_ref, sems
):
    heads, size, width = x_ref.shape
    features = features_ref[...] + dot(turned_ref[1], x_ref[...].reshape(heads * size, width))
    features = features.astype(BF16).astype(F32)
    normed = norm_columns(features).astype(F32).T.astype(BF16)
    channels = placed_ref.shape[1]
    for k in range(8):
        rows = slice(k * width, (k + 1) * width)
        expanded = dot(normed, unpool_ref[:, k * channels : (k + 1) * channels])
        sum_ref[rows, :] = placed_ref[rows, :] + expanded
    parts = sems.shape[0]
    count = rows_ref.shape[0] // parts
    copies = []
    for p in range(parts):

        def move(row, p=p):
            at = p * count + row
            rows_ref[pl.ds(at, 1), :] = sum_ref[pl.ds(place_ref[at], 1), :]

        each_row(count, move)
        mine = pl.ds(p * count, count)
        copies.append(fetch(rows_ref.at[mine, :], out_ref.at[mine, :], sems.at[p]))
    for copy in copies:
        copy.wait()


def shaped(shape, dtype):
    return jax.ShapeDtypeStruct(shape, dtype)


def exchange(value, axes):
    return lax.all_to_all(value, axes, split_axis=0, concat_axis=0, tiled=True)


def shards(
    beads,
    rot_perm,
    pool_ids,
    ball_counts,
    fine_qkv,
    fine_out,
    pool_weight,
    coarse_qkv,
    coarse_out,
    unpool_weight,
):
    own, channels = beads.shape
    both = ("leaf", "sub")
    subs = lax.axis_size("sub")
    devices = lax.axis_size("leaf") * subs
    bucket = own // devices
    nodes = own // 8
    wide = pool_weight.shape[1]
    size = wide // CHEADS
    wanted, slots = call(
        functools.partial(route_kernel, own=own, devices=devices),
        (shaped((devices, 128), jnp.int32), shaped((own // 128, 128), jnp.int32)),
        [vmem()],
        (vmem(), vmem()),
        flops=2 * devices * own * 256,
        nbytes=100000,
        name="route",
    )(rot_perm.reshape(own // 128, 128))
    requested = exchange(wanted.reshape(devices, 1, 128), both).reshape(devices, 128)
    places = call(
        functools.partial(place_kernel, nodes=nodes),
        shaped((own // 128, 128), jnp.int32),
        [vmem()],
        vmem(),
        flops=2 * nodes * own * 256,
        nbytes=20000,
        name="place",
    )(pool_ids.reshape(own // 128, 128))

    slots = slots.reshape(own)
    places = places.reshape(own)
    ball_flops = own * channels * channels * 8 + own * BALL * channels * 16

    after_tree = call(
        first_kernel,
        shaped((own, channels), F32),
        [hbm()] * 3,
        vmem(),
        [
            pltpu.VMEM((2, own // 2, channels), F32),
            pltpu.VMEM((channels, 3 * channels), BF16),
            pltpu.VMEM((channels, channels), BF16),
            pltpu.SemaphoreType.DMA((4,)),
        ],
        flops=ball_flops,
        nbytes=own * channels * 8,
        name="first",
    )(in_hbm(beads), in_hbm(fine_qkv), in_hbm(fine_out))
    answer, named = call(
        functools.partial(answer_kernel, bucket=bucket),
        (shaped((own, channels), BF16), shaped((own // 128, 128), jnp.int32)),
        [vmem(), vmem()],
        (vmem(), vmem()),
        [
            pltpu.VMEM((own, channels), F32),
            pltpu.SMEM((own // 128, 128), jnp.int32),
            pltpu.SemaphoreType.DMA(()),
        ],
        nbytes=own * channels * 6,
        name="answer",
    )(requested, after_tree)
    named = named.reshape(own)
    arrived = exchange(answer.reshape(devices, bucket, channels), both).reshape(own, channels)
    outgoing = call(
        second_kernel,
        shaped((own, channels), BF16),
        [smem()] + [vmem()] * 3,
        vmem(),
        [pltpu.VMEM((own, channels), F32)] * 2 + [pltpu.VMEM((BALL, channels), F32)] * 4,
        flops=ball_flops,
        nbytes=own * channels * 4,
        name="second",
    )(slots, arrived, fine_qkv, fine_out)
    coming = exchange(outgoing.reshape(devices, bucket, channels), both).reshape(own, channels)
    qkv_turned = coarse_qkv.transpose(0, 2, 1)
    out_turned = coarse_out.transpose(0, 2, 1)
    coming, qkv_turned, out_turned = lax.optimization_barrier((coming, qkv_turned, out_turned))
    message, features, placed = call(
        pool_kernel,
        (
            shaped((CHEADS, 3 * size, nodes), BF16),
            shaped((wide, nodes), F32),
            shaped((own, channels), F32),
        ),
        [smem(), smem(), vmem(), hbm(), vmem()],
        (vmem(), vmem(), vmem()),
        [
            pltpu.VMEM((own, channels), F32),
            pltpu.VMEM((own // 2, wide), BF16),
            pltpu.SemaphoreType.DMA(()),
        ],
        flops=2 * nodes * wide * (own // 2 + 3 * wide),
        nbytes=own * channels * 8,
        name="pool",
    )(named, places, coming, in_hbm(pool_weight), qkv_turned)
    for layer in range(2):
        received = exchange(message, "sub")
        attended = call(
            coarse_kernel,
            shaped((subs, size, nodes), BF16),
            [smem(), vmem()],
            vmem(),
            [pltpu.VMEM((subs, nodes, size), BF16), pltpu.VMEM((subs, size + 16, nodes), BF16)]
            + [pltpu.VMEM((1, nodes), F32), pltpu.VMEM((size + 16, nodes), F32)],
            flops=subs * nodes * nodes * 3 * size * 4,
            nbytes=subs * nodes * size * 8,
            name="coarse",
        )(ball_counts, received)
        back = exchange(attended, "sub")
        if layer == 0:
            message, features = call(
                between_kernel,
                (shaped((CHEADS, 3 * size, nodes), BF16), shaped((wide, nodes), F32)),
                [vmem()] * 4,
                (vmem(), vmem()),
                flops=2 * nodes * wide * 4 * wide,
                nbytes=nodes * wide * 8,
                name="between",
            )(back, features, out_turned, qkv_turned)
    return call(
        last_kernel,
        shaped((own, channels), F32),
        [smem()] + [vmem()] * 5,
        hbm(),
        [
            pltpu.VMEM((own, channels), F32),
            pltpu.VMEM((own, channels), F32),
            pltpu.SemaphoreType.DMA((4,)),
        ],
        flops=2 * nodes * wide * 3 * wide,
        nbytes=own * channels * 8,
        name="last",
    )(places, back, features, out_turned, unpool_weight, placed)


def solution(mesh):
    placed = (
        P(("leaf", "sub"), None),
        P(("leaf", "sub")),
        P(("leaf", "sub")),
        P("leaf", None),
        P(),
        P(),
        P(),
        P(),
        P(),
        P(),
    )
    return jax.shard_map(
        shards, mesh=mesh, in_specs=placed, out_specs=P(("leaf", "sub"), None), check_vma=False
    )
```

```python
import functools
import math

import jax
import jax.numpy as jnp
from jax import lax
from jax.experimental import pallas as pl
from jax.experimental.pallas import tpu as pltpu
from jax.sharding import PartitionSpec as P

HEADS = 4
CHEADS = 8
BALL = 256
GRAN = 32
LOG2E = 1.4426950408889634
NEG = -1e30
F32 = jnp.float32
BF16 = jnp.bfloat16


def vmem():
    return pl.BlockSpec(memory_space=pltpu.VMEM)


def smem():
    return pl.BlockSpec(memory_space=pltpu.SMEM)


def hbm():
    return pl.BlockSpec(memory_space=pltpu.HBM)


def in_hbm(value):
    return pltpu.with_memory_space_constraint(value, pltpu.HBM)


def fetch(source, target, sem):
    copy = pltpu.make_async_copy(source, target, sem)
    copy.start()
    return copy


def dot(a, b, dims=((1,), (0,))):
    return lax.dot_general(a, b, (dims, ((), ())), preferred_element_type=F32)


def call(kernel, out_shape, in_specs, out_specs, scratch=(), flops=0, nbytes=0, name=None, mib=16):
    return pl.pallas_call(
        kernel,
        out_shape=out_shape,
        in_specs=in_specs,
        out_specs=out_specs,
        scratch_shapes=list(scratch),
        cost_estimate=pl.CostEstimate(flops=flops, bytes_accessed=nbytes, transcendentals=0),
        compiler_params=pltpu.CompilerParams(vmem_limit_bytes=mib << 20),
        name=name,
    )


def ranks(classes, count):
    step = 256
    tri = (
        lax.broadcasted_iota(jnp.int32, (step, step), 0)
        <= lax.broadcasted_iota(jnp.int32, (step, step), 1)
    )
    tri = jnp.where(tri, 1.0, 0.0).astype(BF16)
    names = lax.broadcasted_iota(jnp.int32, (count, step), 0)
    carried = jnp.zeros((count, 1), F32)
    hots, found = [], []
    for row in classes:
        hot = jnp.where(names == row, 1.0, 0.0)
        hot16 = hot.astype(BF16)
        running = dot(hot16, tri) + carried
        found.append((jnp.sum(hot * running, axis=0, keepdims=True) - 1.0).astype(jnp.int32))
        hots.append(hot16)
        carried = running[:, step - 1 : step]
    return hots, found


def row_pairs(ref):
    return [
        jnp.concatenate([ref[2 * r : 2 * r + 1, :], ref[2 * r + 1 : 2 * r + 2, :]], axis=1)
        for r in range(ref.shape[0] // 2)
    ]


def store_pair(ref, r, value):
    ref[2 * r : 2 * r + 1, :] = value[:, :128]
    ref[2 * r + 1 : 2 * r + 2, :] = value[:, 128:]


def route_kernel(rot_ref, wanted_ref, slot_ref, *, own, devices):
    bucket = own // devices
    named = row_pairs(rot_ref)
    own_bits = own.bit_length() - 1
    dest = [row >> own_bits for row in named]
    hots, found = ranks(dest, devices)
    lanes = lax.broadcasted_iota(jnp.int32, (bucket, 256), 0)
    total = jnp.zeros((devices, 2 * bucket), F32)
    for r, row in enumerate(named):
        store_pair(slot_ref, r, dest[r] * bucket + found[r])
        local = row & (own - 1)
        here = lanes == found[r]
        high = jnp.where(here, (local >> 6).astype(F32), 0.0)
        low = jnp.where(here, (local & 63).astype(F32), 0.0)
        parts = jnp.concatenate([high, low], axis=0).astype(BF16)
        total = total + dot(hots[r], parts, ((1,), (1,)))
    wanted = total[:, :bucket] * 64.0 + total[:, bucket:]
    wanted_ref[...] = jnp.zeros_like(wanted_ref)
    wanted_ref[:, :bucket] = wanted.astype(jnp.int32)


def place_kernel(pool_ref, place_ref, *, nodes):
    node = [row & (nodes - 1) for row in row_pairs(pool_ref)]
    _, found = ranks(node, nodes)
    for r in range(len(node)):
        store_pair(place_ref, r, found[r] * nodes + node[r])


def norm_rows(x):
    centre = x - jnp.mean(x, axis=-1, keepdims=True)
    spread = jnp.mean(centre * centre, axis=-1, keepdims=True)
    return (centre * lax.rsqrt(spread + 1e-5)).astype(BF16)


def norm_columns(x):
    centre = x - jnp.mean(x, axis=0, keepdims=True)
    spread = jnp.mean(centre * centre, axis=0, keepdims=True)
    return (centre * lax.rsqrt(spread + 1e-5)).astype(BF16)


def ball(x, qkv_weight, out_weight):
    channels = x.shape[1]
    size = channels // HEADS
    normed = norm_rows(x)
    queries = dot(normed, qkv_weight[:, :channels]).astype(BF16)
    keys = dot(normed, qkv_weight[:, channels : 2 * channels]).astype(BF16)
    values = dot(normed, qkv_weight[:, 2 * channels :]).astype(BF16)
    values = jnp.concatenate([values, jnp.ones_like(values)], axis=1)
    head_of = lax.broadcasted_iota(jnp.int32, (1, channels), 1) // size
    summed = total = None
    for head in range(HEADS):
        mine = head_of == head
        scores = dot(jnp.where(mine, queries, jnp.zeros_like(queries)), keys, ((1,), (1,)))
        most = jnp.max(scores, axis=1, keepdims=True)
        weights = jnp.exp2((scores - most) * (LOG2E / math.sqrt(size))).astype(BF16)
        both = dot(weights, values)
        part, weight = both[:, :channels], both[:, channels:]
        summed = part if head == 0 else jnp.where(mine, part, summed)
        total = weight if head == 0 else jnp.where(mine, weight, total)
    return x + dot((summed / total).astype(BF16), out_weight)


def first_kernel(x_ref, qkv_ref, out_ref, y_ref, held_ref, qkv_held, out_held, sems):
    rows = held_ref.shape[1]
    weights = [fetch(qkv_ref.at[0], qkv_held, sems.at[0]), fetch(out_ref.at[0], out_held, sems.at[1])]
    parts = [
        fetch(x_ref.at[pl.ds(p * rows, rows), :], held_ref.at[p], sems.at[2 + p])
        for p in range(held_ref.shape[0])
    ]
    for copy in weights:
        copy.wait()
    for p, copy in enumerate(parts):
        copy.wait()
        for j in range(rows // BALL):
            mine = slice(j * BALL, (j + 1) * BALL)
            at = p * rows + j * BALL
            y_ref[at : at + BALL, :] = ball(held_ref[p, mine, :], qkv_held[...], out_held[...])


def each_row(count, move):
    together = min(count, 128)

    def some(step, _):
        for j in range(together):
            move(step * together + j)
        return 0

    lax.fori_loop(0, count // together, some, 0)


def answer_kernel(wanted_ref, x_ref, out_ref, named_ref, rows_ref, index_ref, sem, *, bucket):
    devices = wanted_ref.shape[0]
    per_row = 128 // bucket
    named_ref[...] = jnp.concatenate(
        [wanted_ref[pl.ds(i, devices // per_row, stride=per_row), :][:, :bucket] for i in range(per_row)],
        axis=1,
    )
    fetch(named_ref, index_ref, sem).wait()

    def some(step, _):
        for j in range(128):
            rows_ref[pl.ds(step * 128 + j, 1), :] = x_ref[pl.ds(index_ref[step, j], 1), :]
        return 0

    lax.fori_loop(0, index_ref.shape[0], some, 0)
    out_ref[...] = rows_ref[...].astype(BF16)


def second_kernel(slot_ref, x_ref, qkv_ref, out_ref, y_ref, from_ref, to_ref, in0, in1, out0, out1):
    ins, outs = (in0, in1), (out0, out1)
    count = x_ref.shape[0] // BALL
    from_ref[...] = x_ref[...].astype(F32)

    def take_first(row):
        in0[pl.ds(row, 1), :] = from_ref[pl.ds(slot_ref[row], 1), :]

    def give_last(row):
        slot = slot_ref[(count - 1) * BALL + row]
        to_ref[pl.ds(slot, 1), :] = outs[(count - 1) % 2][pl.ds(row, 1), :]

    each_row(BALL, take_first)
    for at in range(count):
        if at + 1 < count:
            for j in range(BALL):
                slot = slot_ref[(at + 1) * BALL + j]
                ins[(at + 1) % 2][j : j + 1, :] = from_ref[pl.ds(slot, 1), :]
        outs[at % 2][...] = ball(ins[at % 2][...], qkv_ref[1], out_ref[1])
        if at:
            for j in range(BALL):
                slot = slot_ref[(at - 1) * BALL + j]
                to_ref[pl.ds(slot, 1), :] = outs[(at - 1) % 2][j : j + 1, :]
    each_row(BALL, give_last)
    y_ref[...] = to_ref[...].astype(BF16)


def place_in_message(message_ref, target, rows, value):
    me = lax.axis_index("sub")
    other = (target & 1) ^ (me & 1)
    ahead = ((target >> 1) - (me >> 1)) & 3
    message_ref[other, ahead, rows, :] = value


def received_blocks(message_ref, swapped_ref, shifted_refs):
    me = lax.axis_index("sub")
    for back in range(4):
        for other in range(2):
            source = ((((me >> 1) - back) & 3) << 1) + ((me & 1) ^ other)
            if back:
                yield source, shifted_refs[back - 1].at[other]
            elif other:
                yield source, swapped_ref.at[0]
            else:
                yield source, message_ref.at[0, 0]


def send_projected(features, weight, message_ref):
    normed = norm_columns(features)
    channels = features.shape[0]
    size = channels // CHEADS
    for part in range(3):
        projected = dot(weight[part * channels : (part + 1) * channels, :], normed).astype(BF16)
        for head in range(CHEADS):
            place_in_message(
                message_ref,
                head,
                slice(part * size, (part + 1) * size),
                projected[head * size : (head + 1) * size],
            )


def pool_kernel(
    named_ref, place_ref, x_ref, pool_ref, qkv_ref, message_ref, pooled_ref, placed_ref, from_ref, held_ref, sem
):
    weight_copy = fetch(pool_ref, held_ref, sem)
    from_ref[...] = x_ref[...].astype(F32)

    def move(slot):
        placed_ref[pl.ds(place_ref[named_ref[slot]], 1), :] = from_ref[pl.ds(slot, 1), :]

    each_row(from_ref.shape[0], move)
    nodes = x_ref.shape[0] // 8
    channels = x_ref.shape[1]
    weight_copy.wait()
    pooled = None
    for k in range(8):
        part = dot(
            placed_ref[k * nodes : (k + 1) * nodes, :].astype(BF16),
            held_ref[k * channels : (k + 1) * channels, :],
        )
        pooled = part if pooled is None else pooled + part
    pooled = pooled.astype(BF16).astype(F32).T
    pooled_ref[...] = pooled
    send_projected(pooled, qkv_ref[0], message_ref)


def coarse_kernel(
    counts_ref,
    message_ref,
    swapped_ref,
    one_ref,
    two_ref,
    three_ref,
    out_ref,
    queries_ref,
    keys_ref,
    values_ref,
    most_ref,
    total_ref,
):
    tiles, size, width = queries_ref.shape
    per_tile = width // GRAN
    top = 4
    scale = LOG2E / math.sqrt(size)
    ones = jnp.ones((16, width), BF16)
    for t, block_ref in received_blocks(message_ref, swapped_ref, (one_ref, two_ref, three_ref)):
        queries_ref[t] = block_ref[:size, :]
        keys_ref[t] = block_ref[size : 2 * size, :].astype(F32).T.astype(BF16)
        values_ref[t] = jnp.concatenate([block_ref[2 * size :, :], ones], axis=0)
    edges = [counts_ref[0, 0]]
    for e in range(1, counts_ref.shape[1] - 1):
        edges.append(edges[-1] + counts_ref[0, e])
    lane_block = lax.broadcasted_iota(jnp.int32, (1, width), 1) >> (GRAN.bit_length() - 1)
    tile_bits = per_tile.bit_length() - 1

    def ball_around(block):
        begin, end = 0, tiles * per_tile
        for edge in edges:
            begin = jnp.where(edge <= block, edge, begin)
        for edge in reversed(edges):
            end = jnp.where(edge > block, edge, end)
        return begin, end

    def one(tile, _):
        queries = queries_ref[tile]
        begin, end = ball_around(tile * per_tile + lane_block)
        low = ball_around(tile * per_tile)[0] >> tile_bits
        high = (ball_around(tile * per_tile + per_tile - 1)[1] - 1) >> tile_bits

        def scored(chunk):
            scores = dot(keys_ref[chunk], queries)
            masked = []
            for g in range(per_tile):
                block = chunk * per_tile + g
                seen = jnp.logical_and(block >= begin, block < end)
                masked.append(jnp.where(seen, scores[g * GRAN : (g + 1) * GRAN], NEG))
            return jnp.concatenate(masked, axis=0)

        def several(chunk, count, carried):
            scores = [scored(chunk + c) for c in range(count)]
            now = most = most_ref[...] if carried else None
            for s in scores:
                here = jnp.max(s, axis=0, keepdims=True)
                now = here if now is None else jnp.maximum(now, here)
            total = total_ref[...] * jnp.exp2((most - now) * scale) if carried else None
            for c, s in enumerate(scores):
                part = dot(values_ref[chunk + c], jnp.exp2((s - now) * scale).astype(BF16))
                total = part if total is None else total + part
            most_ref[...] = now
            total_ref[...] = total

        number = high - low + 1
        head = jnp.where(number <= top, number, jnp.where(number == top + 1, top - 1, top))
        for count in range(1, top + 1):

            @pl.when(head == count)
            def _(count=count):
                several(low, count, False)

        def more(step, _):
            chunk = low + head + step * 2
            left = high - chunk + 1

            @pl.when(left >= 2)
            def _():
                several(chunk, 2, True)

            @pl.when(left == 1)
            def _():
                several(chunk, 1, True)

            return 0

        lax.fori_loop(0, (number - head + 1) >> 1, more, 0)
        total = total_ref[...]
        place_in_message(out_ref, tile, slice(0, size), (total[:size] / total[size : size + 1]).astype(BF16))
        return 0

    lax.fori_loop(0, tiles, one, 0)


def attended_heads(message_ref, swapped_ref, shifted_refs, heads_ref):
    heads, size, width = heads_ref.shape
    for head, block_ref in received_blocks(message_ref, swapped_ref, shifted_refs):
        heads_ref[head] = block_ref[...]
    return heads_ref[...].reshape(heads * size, width)


def between_kernel(
    back_ref,
    swapped_ref,
    one_ref,
    two_ref,
    three_ref,
    features_ref,
    turned_ref,
    qkv_ref,
    message_ref,
    next_ref,
    heads_ref,
):
    attended = attended_heads(back_ref, swapped_ref, (one_ref, two_ref, three_ref), heads_ref)
    features = features_ref[...] + dot(turned_ref[0], attended)
    next_ref[...] = features
    send_projected(features, qkv_ref[1], message_ref)


def last_kernel(
    place_ref,
    back_ref,
    swapped_ref,
    one_ref,
    two_ref,
    three_ref,
    features_ref,
    turned_ref,
    unpool_ref,
    placed_ref,
    out_ref,
    sum_ref,
    rows_ref,
    heads_ref,
    sems,
):
    attended = attended_heads(back_ref, swapped_ref, (one_ref, two_ref, three_ref), heads_ref)
    width = attended.shape[1]
    features = features_ref[...] + dot(turned_ref[1], attended)
    features = features.astype(BF16).astype(F32)
    normed = norm_columns(features).astype(F32).T.astype(BF16)
    channels = placed_ref.shape[1]
    for k in range(8):
        rows = slice(k * width, (k + 1) * width)
        expanded = dot(normed, unpool_ref[:, k * channels : (k + 1) * channels])
        sum_ref[rows, :] = placed_ref[rows, :] + expanded
    parts = sems.shape[0]
    count = rows_ref.shape[0] // parts
    copies = []
    for p in range(parts):

        def move(row, p=p):
            at = p * count + row
            rows_ref[pl.ds(at, 1), :] = sum_ref[pl.ds(place_ref[at], 1), :]

        each_row(count, move)
        mine = pl.ds(p * count, count)
        copies.append(fetch(rows_ref.at[mine, :], out_ref.at[mine, :], sems.at[p]))
    for copy in copies:
        copy.wait()


def shaped(shape, dtype):
    return jax.ShapeDtypeStruct(shape, dtype)


def exchange(value, axes):
    return lax.all_to_all(value, axes, split_axis=0, concat_axis=0, tiled=True)


def exchange_sub(message):
    ring = lax.axis_size("sub")
    swapped = lax.ppermute(message[1], "sub", [(i, i ^ 1) for i in range(ring)])
    both = jnp.stack([message[0], swapped], axis=1)
    shifted = {}
    for ahead in (2, 1, 3):
        pairs = [(i, (i + 2 * ahead) % ring) for i in range(ring)]
        shifted[ahead] = lax.ppermute(both[ahead], "sub", pairs)
    return message, swapped, shifted[1], shifted[2], shifted[3]


def shards(
    beads,
    rot_perm,
    pool_ids,
    ball_counts,
    fine_qkv,
    fine_out,
    pool_weight,
    coarse_qkv,
    coarse_out,
    unpool_weight,
):
    own, channels = beads.shape
    both = ("leaf", "sub")
    subs = lax.axis_size("sub")
    devices = lax.axis_size("leaf") * subs
    bucket = own // devices
    nodes = own // 8
    wide = pool_weight.shape[1]
    size = wide // CHEADS
    wanted, slots = call(
        functools.partial(route_kernel, own=own, devices=devices),
        (shaped((devices, 128), jnp.int32), shaped((own // 128, 128), jnp.int32)),
        [vmem()],
        (vmem(), vmem()),
        flops=2 * devices * own * 256,
        nbytes=100000,
        name="route",
    )(rot_perm.reshape(own // 128, 128))
    requested = exchange(wanted.reshape(devices, 1, 128), both).reshape(devices, 128)
    places = call(
        functools.partial(place_kernel, nodes=nodes),
        shaped((own // 128, 128), jnp.int32),
        [vmem()],
        vmem(),
        flops=2 * nodes * own * 256,
        nbytes=20000,
        name="place",
    )(pool_ids.reshape(own // 128, 128))

    slots = slots.reshape(own)
    places = places.reshape(own)
    ball_flops = own * channels * channels * 8 + own * BALL * channels * 16

    after_tree = call(
        first_kernel,
        shaped((own, channels), F32),
        [hbm()] * 3,
        vmem(),
        [
            pltpu.VMEM((2, own // 2, channels), F32),
            pltpu.VMEM((channels, 3 * channels), BF16),
            pltpu.VMEM((channels, channels), BF16),
            pltpu.SemaphoreType.DMA((4,)),
        ],
        flops=ball_flops,
        nbytes=own * channels * 8,
        name="first",
    )(in_hbm(beads), in_hbm(fine_qkv), in_hbm(fine_out))
    answer, named = call(
        functools.partial(answer_kernel, bucket=bucket),
        (shaped((own, channels), BF16), shaped((own // 128, 128), jnp.int32)),
        [vmem(), vmem()],
        (vmem(), vmem()),
        [
            pltpu.VMEM((own, channels), F32),
            pltpu.SMEM((own // 128, 128), jnp.int32),
            pltpu.SemaphoreType.DMA(()),
        ],
        nbytes=own * channels * 6,
        name="answer",
    )(requested, after_tree)
    named = named.reshape(own)
    arrived = exchange(answer.reshape(devices, bucket, channels), both).reshape(own, channels)
    outgoing = call(
        second_kernel,
        shaped((own, channels), BF16),
        [smem()] + [vmem()] * 3,
        vmem(),
        [pltpu.VMEM((own, channels), F32)] * 2 + [pltpu.VMEM((BALL, channels), F32)] * 4,
        flops=ball_flops,
        nbytes=own * channels * 4,
        name="second",
    )(slots, arrived, fine_qkv, fine_out)
    coming = exchange(outgoing.reshape(devices, bucket, channels), both).reshape(own, channels)
    qkv_turned = coarse_qkv.transpose(0, 2, 1)
    out_turned = coarse_out.transpose(0, 2, 1)
    coming, qkv_turned, out_turned = lax.optimization_barrier((coming, qkv_turned, out_turned))
    message, features, placed = call(
        pool_kernel,
        (
            shaped((2, subs // 2, 3 * size, nodes), BF16),
            shaped((wide, nodes), F32),
            shaped((own, channels), F32),
        ),
        [smem(), smem(), vmem(), hbm(), vmem()],
        (vmem(), vmem(), vmem()),
        [
            pltpu.VMEM((own, channels), F32),
            pltpu.VMEM((own // 2, wide), BF16),
            pltpu.SemaphoreType.DMA(()),
        ],
        flops=2 * nodes * wide * (own // 2 + 3 * wide),
        nbytes=own * channels * 8,
        name="pool",
    )(named, places, coming, in_hbm(pool_weight), qkv_turned)
    for layer in range(2):
        received = exchange_sub(message)
        attended = call(
            coarse_kernel,
            shaped((2, subs // 2, size, nodes), BF16),
            [smem()] + [vmem()] * 5,
            vmem(),
            [pltpu.VMEM((subs, size, nodes), BF16), pltpu.VMEM((subs, nodes, size), BF16), pltpu.VMEM((subs, size + 16, nodes), BF16)]
            + [pltpu.VMEM((1, nodes), F32), pltpu.VMEM((size + 16, nodes), F32)],
            flops=subs * nodes * nodes * 3 * size * 4,
            nbytes=subs * nodes * size * 8,
            name="coarse",
        )(ball_counts, *received)
        back = exchange_sub(attended)
        if layer == 0:
            message, features = call(
                between_kernel,
                (shaped((2, subs // 2, 3 * size, nodes), BF16), shaped((wide, nodes), F32)),
                [vmem()] * 8,
                (vmem(), vmem()),
                [pltpu.VMEM((subs, size, nodes), BF16)],
                flops=2 * nodes * wide * 4 * wide,
                nbytes=nodes * wide * 8,
                name="between",
            )(*back, features, out_turned, qkv_turned)
    return call(
        last_kernel,
        shaped((own, channels), F32),
        [smem()] + [vmem()] * 9,
        hbm(),
        [
            pltpu.VMEM((own, channels), F32),
            pltpu.VMEM((own, channels), F32),
            pltpu.VMEM((subs, size, nodes), BF16),
            pltpu.SemaphoreType.DMA((4,)),
        ],
        flops=2 * nodes * wide * 3 * wide,
        nbytes=own * channels * 8,
        name="last",
    )(places, *back, features, out_turned, unpool_weight, placed)


def solution(mesh):
    placed = (
        P(("leaf", "sub"), None),
        P(("leaf", "sub")),
        P(("leaf", "sub")),
        P("leaf", None),
        P(),
        P(),
        P(),
        P(),
        P(),
        P(),
    )
    return jax.shard_map(
        shards, mesh=mesh, in_specs=placed, out_specs=P(("leaf", "sub"), None), check_vma=False
    )
```

```python
import functools
import math

import jax
import jax.numpy as jnp
from jax import lax
from jax.experimental import pallas as pl
from jax.experimental.pallas import tpu as pltpu
from jax.sharding import PartitionSpec as P

HEADS = 4
CHEADS = 8
BALL = 256
GRAN = 32
LOG2E = 1.4426950408889634
NEG = -1e30
F32 = jnp.float32
BF16 = jnp.bfloat16


def vmem():
    return pl.BlockSpec(memory_space=pltpu.VMEM)


def smem():
    return pl.BlockSpec(memory_space=pltpu.SMEM)


def hbm():
    return pl.BlockSpec(memory_space=pltpu.HBM)


def in_hbm(value):
    return pltpu.with_memory_space_constraint(value, pltpu.HBM)


def fetch(source, target, sem):
    copy = pltpu.make_async_copy(source, target, sem)
    copy.start()
    return copy


def dot(a, b, dims=((1,), (0,))):
    return lax.dot_general(a, b, (dims, ((), ())), preferred_element_type=F32)


def call(kernel, out_shape, in_specs, out_specs, scratch=(), flops=0, nbytes=0, name=None, mib=16):
    return pl.pallas_call(
        kernel,
        out_shape=out_shape,
        in_specs=in_specs,
        out_specs=out_specs,
        scratch_shapes=list(scratch),
        cost_estimate=pl.CostEstimate(flops=flops, bytes_accessed=nbytes, transcendentals=0),
        compiler_params=pltpu.CompilerParams(vmem_limit_bytes=mib << 20),
        name=name,
    )


def ranks(classes, count):
    step = 256
    tri = (
        lax.broadcasted_iota(jnp.int32, (step, step), 0)
        <= lax.broadcasted_iota(jnp.int32, (step, step), 1)
    )
    tri = jnp.where(tri, 1.0, 0.0).astype(BF16)
    names = lax.broadcasted_iota(jnp.int32, (count, step), 0)
    carried = jnp.zeros((count, 1), F32)
    hots, found = [], []
    for row in classes:
        hot = jnp.where(names == row, 1.0, 0.0)
        hot16 = hot.astype(BF16)
        running = dot(hot16, tri) + carried
        found.append((jnp.sum(hot * running, axis=0, keepdims=True) - 1.0).astype(jnp.int32))
        hots.append(hot16)
        carried = running[:, step - 1 : step]
    return hots, found


def row_pairs(ref):
    return [
        jnp.concatenate([ref[2 * r : 2 * r + 1, :], ref[2 * r + 1 : 2 * r + 2, :]], axis=1)
        for r in range(ref.shape[0] // 2)
    ]


def store_pair(ref, r, value):
    ref[2 * r : 2 * r + 1, :] = value[:, :128]
    ref[2 * r + 1 : 2 * r + 2, :] = value[:, 128:]


def route_kernel(rot_ref, wanted_ref, slot_ref, *, own, devices):
    bucket = own // devices
    named = row_pairs(rot_ref)
    own_bits = own.bit_length() - 1
    dest = [row >> own_bits for row in named]
    hots, found = ranks(dest, devices)
    lanes = lax.broadcasted_iota(jnp.int32, (bucket, 256), 0)
    total = jnp.zeros((devices, 2 * bucket), F32)
    for r, row in enumerate(named):
        store_pair(slot_ref, r, dest[r] * bucket + found[r])
        local = row & (own - 1)
        here = lanes == found[r]
        high = jnp.where(here, (local >> 6).astype(F32), 0.0)
        low = jnp.where(here, (local & 63).astype(F32), 0.0)
        parts = jnp.concatenate([high, low], axis=0).astype(BF16)
        total = total + dot(hots[r], parts, ((1,), (1,)))
    wanted = total[:, :bucket] * 64.0 + total[:, bucket:]
    wanted_ref[...] = jnp.zeros_like(wanted_ref)
    wanted_ref[:, :bucket] = wanted.astype(jnp.int32)


def place_kernel(pool_ref, place_ref, *, nodes):
    node = [row & (nodes - 1) for row in row_pairs(pool_ref)]
    _, found = ranks(node, nodes)
    for r in range(len(node)):
        store_pair(place_ref, r, found[r] * nodes + node[r])


def norm_rows(x):
    centre = x - jnp.mean(x, axis=-1, keepdims=True)
    spread = jnp.mean(centre * centre, axis=-1, keepdims=True)
    return (centre * lax.rsqrt(spread + 1e-5)).astype(BF16)


def norm_columns(x):
    centre = x - jnp.mean(x, axis=0, keepdims=True)
    spread = jnp.mean(centre * centre, axis=0, keepdims=True)
    return (centre * lax.rsqrt(spread + 1e-5)).astype(BF16)


def ball(x, qkv_weight, out_weight):
    channels = x.shape[1]
    size = channels // HEADS
    normed = norm_rows(x)
    queries = dot(normed, qkv_weight[:, :channels]).astype(BF16)
    keys = dot(normed, qkv_weight[:, channels : 2 * channels]).astype(BF16)
    values = dot(normed, qkv_weight[:, 2 * channels :]).astype(BF16)
    values = jnp.concatenate([values, jnp.ones_like(values)], axis=1)
    head_of = lax.broadcasted_iota(jnp.int32, (1, channels), 1) // size
    summed = total = None
    for head in range(HEADS):
        mine = head_of == head
        scores = dot(jnp.where(mine, queries, jnp.zeros_like(queries)), keys, ((1,), (1,)))
        most = jnp.max(scores, axis=1, keepdims=True)
        weights = jnp.exp2((scores - most) * (LOG2E / math.sqrt(size))).astype(BF16)
        both = dot(weights, values)
        part, weight = both[:, :channels], both[:, channels:]
        summed = part if head == 0 else jnp.where(mine, part, summed)
        total = weight if head == 0 else jnp.where(mine, weight, total)
    return x + dot((summed / total).astype(BF16), out_weight)


def first_kernel(x_ref, qkv_ref, out_ref, y_ref, held_ref, qkv_held, out_held, sems):
    rows = held_ref.shape[1]
    weights = [fetch(qkv_ref.at[0], qkv_held, sems.at[0]), fetch(out_ref.at[0], out_held, sems.at[1])]
    parts = [
        fetch(x_ref.at[pl.ds(p * rows, rows), :], held_ref.at[p], sems.at[2 + p])
        for p in range(held_ref.shape[0])
    ]
    for copy in weights:
        copy.wait()
    for p, copy in enumerate(parts):
        copy.wait()
        for j in range(rows // BALL):
            mine = slice(j * BALL, (j + 1) * BALL)
            at = p * rows + j * BALL
            y_ref[at : at + BALL, :] = ball(held_ref[p, mine, :], qkv_held[...], out_held[...])


def each_row(count, move):
    together = min(count, 128)

    def some(step, _):
        for j in range(together):
            move(step * together + j)
        return 0

    lax.fori_loop(0, count // together, some, 0)


def answer_kernel(wanted_ref, x_ref, out_ref, named_ref, rows_ref, index_ref, sem, *, bucket):
    devices = wanted_ref.shape[0]
    per_row = 128 // bucket
    named_ref[...] = jnp.concatenate(
        [wanted_ref[pl.ds(i, devices // per_row, stride=per_row), :][:, :bucket] for i in range(per_row)],
        axis=1,
    )
    fetch(named_ref, index_ref, sem).wait()

    def some(step, _):
        for j in range(128):
            rows_ref[pl.ds(step * 128 + j, 1), :] = x_ref[pl.ds(index_ref[step, j], 1), :]
        return 0

    lax.fori_loop(0, index_ref.shape[0], some, 0)
    out_ref[...] = rows_ref[...].astype(BF16)


def second_kernel(slot_ref, x_ref, qkv_ref, out_ref, y_ref, from_ref, to_ref, in0, in1, out0, out1):
    ins, outs = (in0, in1), (out0, out1)
    count = x_ref.shape[0] // BALL
    from_ref[...] = x_ref[...].astype(F32)

    def take_first(row):
        in0[pl.ds(row, 1), :] = from_ref[pl.ds(slot_ref[row], 1), :]

    def give_last(row):
        slot = slot_ref[(count - 1) * BALL + row]
        to_ref[pl.ds(slot, 1), :] = outs[(count - 1) % 2][pl.ds(row, 1), :]

    each_row(BALL, take_first)
    for at in range(count):
        if at + 1 < count:
            for j in range(BALL):
                slot = slot_ref[(at + 1) * BALL + j]
                ins[(at + 1) % 2][j : j + 1, :] = from_ref[pl.ds(slot, 1), :]
        outs[at % 2][...] = ball(ins[at % 2][...], qkv_ref[1], out_ref[1])
        if at:
            for j in range(BALL):
                slot = slot_ref[(at - 1) * BALL + j]
                to_ref[pl.ds(slot, 1), :] = outs[(at - 1) % 2][j : j + 1, :]
    each_row(BALL, give_last)
    y_ref[...] = to_ref[...].astype(BF16)


def place_in_message(message_ref, target, rows, value):
    me = lax.axis_index("sub")
    other = (target & 1) ^ (me & 1)
    ahead = ((target >> 1) - (me >> 1)) & 3
    message_ref[other, ahead, rows, :] = value


def received_blocks(message_ref, swapped_ref, shifted_refs):
    me = lax.axis_index("sub")
    for back in range(4):
        for other in range(2):
            source = ((((me >> 1) - back) & 3) << 1) + ((me & 1) ^ other)
            if back:
                yield source, shifted_refs[back - 1].at[other]
            elif other:
                yield source, swapped_ref.at[0]
            else:
                yield source, message_ref.at[0, 0]


def send_projected(features, weight, message_ref):
    normed = norm_columns(features)
    channels = features.shape[0]
    size = channels // CHEADS
    for part in range(3):
        projected = dot(weight[part * channels : (part + 1) * channels, :], normed).astype(BF16)
        for head in range(CHEADS):
            place_in_message(
                message_ref,
                head,
                slice(part * size, (part + 1) * size),
                projected[head * size : (head + 1) * size],
            )


def pool_kernel(
    named_ref, place_ref, x_ref, pool_ref, qkv_ref, message_ref, pooled_ref, placed_ref, from_ref, held_ref, sem
):
    weight_copy = fetch(pool_ref, held_ref, sem)
    from_ref[...] = x_ref[...].astype(F32)

    def move(slot):
        placed_ref[pl.ds(place_ref[named_ref[slot]], 1), :] = from_ref[pl.ds(slot, 1), :]

    each_row(from_ref.shape[0], move)
    nodes = x_ref.shape[0] // 8
    channels = x_ref.shape[1]
    weight_copy.wait()
    pooled = None
    for k in range(8):
        part = dot(
            placed_ref[k * nodes : (k + 1) * nodes, :].astype(BF16),
            held_ref[k * channels : (k + 1) * channels, :],
        )
        pooled = part if pooled is None else pooled + part
    pooled = pooled.astype(BF16).astype(F32).T
    pooled_ref[...] = pooled
    send_projected(pooled, qkv_ref[0], message_ref)


def coarse_kernel(
    counts_ref,
    message_ref,
    swapped_ref,
    three_ref,
    one_ref,
    two_ref,
    out_ref,
    queries_ref,
    keys_ref,
    values_ref,
    most_ref,
    total_ref,
):
    tiles, size, width = queries_ref.shape
    per_tile = width // GRAN
    top = 4
    scale = LOG2E / math.sqrt(size)
    ones = jnp.ones((16, width), BF16)
    for t, block_ref in received_blocks(message_ref, swapped_ref, (one_ref, two_ref, three_ref)):
        queries_ref[t] = block_ref[:size, :]
        keys_ref[t] = block_ref[size : 2 * size, :].astype(F32).T.astype(BF16)
        values_ref[t] = jnp.concatenate([block_ref[2 * size :, :], ones], axis=0)
    edges = [counts_ref[0, 0]]
    for e in range(1, counts_ref.shape[1] - 1):
        edges.append(edges[-1] + counts_ref[0, e])
    lane_block = lax.broadcasted_iota(jnp.int32, (1, width), 1) >> (GRAN.bit_length() - 1)
    tile_bits = per_tile.bit_length() - 1

    def ball_around(block):
        begin, end = 0, tiles * per_tile
        for edge in edges:
            begin = jnp.where(edge <= block, edge, begin)
        for edge in reversed(edges):
            end = jnp.where(edge > block, edge, end)
        return begin, end

    def one(tile, _):
        queries = queries_ref[tile]
        begin, end = ball_around(tile * per_tile + lane_block)
        low = ball_around(tile * per_tile)[0] >> tile_bits
        high = (ball_around(tile * per_tile + per_tile - 1)[1] - 1) >> tile_bits

        def scored(chunk):
            scores = dot(keys_ref[chunk], queries)
            masked = []
            for g in range(per_tile):
                block = chunk * per_tile + g
                seen = jnp.logical_and(block >= begin, block < end)
                masked.append(jnp.where(seen, scores[g * GRAN : (g + 1) * GRAN], NEG))
            return jnp.concatenate(masked, axis=0)

        def several(chunk, count, carried):
            scores = [scored(chunk + c) for c in range(count)]
            now = most = most_ref[...] if carried else None
            for s in scores:
                here = jnp.max(s, axis=0, keepdims=True)
                now = here if now is None else jnp.maximum(now, here)
            total = total_ref[...] * jnp.exp2((most - now) * scale) if carried else None
            for c, s in enumerate(scores):
                part = dot(values_ref[chunk + c], jnp.exp2((s - now) * scale).astype(BF16))
                total = part if total is None else total + part
            most_ref[...] = now
            total_ref[...] = total

        number = high - low + 1
        head = jnp.where(number <= top, number, jnp.where(number == top + 1, top - 1, top))
        for count in range(1, top + 1):

            @pl.when(head == count)
            def _(count=count):
                several(low, count, False)

        def more(step, _):
            chunk = low + head + step * 2
            left = high - chunk + 1

            @pl.when(left >= 2)
            def _():
                several(chunk, 2, True)

            @pl.when(left == 1)
            def _():
                several(chunk, 1, True)

            return 0

        lax.fori_loop(0, (number - head + 1) >> 1, more, 0)
        total = total_ref[...]
        place_in_message(out_ref, tile, slice(0, size), (total[:size] / total[size : size + 1]).astype(BF16))
        return 0

    lax.fori_loop(0, tiles, one, 0)


def attended_heads(message_ref, swapped_ref, shifted_refs, heads_ref):
    heads, size, width = heads_ref.shape
    for head, block_ref in received_blocks(message_ref, swapped_ref, shifted_refs):
        heads_ref[head] = block_ref[...]
    return heads_ref[...].reshape(heads * size, width)


def between_kernel(
    back_ref,
    swapped_ref,
    three_ref,
    one_ref,
    two_ref,
    features_ref,
    turned_ref,
    qkv_ref,
    message_ref,
    next_ref,
    heads_ref,
):
    attended = attended_heads(back_ref, swapped_ref, (one_ref, two_ref, three_ref), heads_ref)
    features = features_ref[...] + dot(turned_ref[0], attended)
    next_ref[...] = features
    send_projected(features, qkv_ref[1], message_ref)


def last_kernel(
    place_ref,
    back_ref,
    swapped_ref,
    three_ref,
    one_ref,
    two_ref,
    features_ref,
    turned_ref,
    unpool_ref,
    placed_ref,
    out_ref,
    sum_ref,
    rows_ref,
    heads_ref,
    sems,
):
    attended = attended_heads(back_ref, swapped_ref, (one_ref, two_ref, three_ref), heads_ref)
    width = attended.shape[1]
    features = features_ref[...] + dot(turned_ref[1], attended)
    features = features.astype(BF16).astype(F32)
    normed = norm_columns(features).astype(F32).T.astype(BF16)
    channels = placed_ref.shape[1]
    for k in range(8):
        rows = slice(k * width, (k + 1) * width)
        expanded = dot(normed, unpool_ref[:, k * channels : (k + 1) * channels])
        sum_ref[rows, :] = placed_ref[rows, :] + expanded
    parts = sems.shape[0]
    count = rows_ref.shape[0] // parts
    copies = []
    for p in range(parts):

        def move(row, p=p):
            at = p * count + row
            rows_ref[pl.ds(at, 1), :] = sum_ref[pl.ds(place_ref[at], 1), :]

        each_row(count, move)
        mine = pl.ds(p * count, count)
        copies.append(fetch(rows_ref.at[mine, :], out_ref.at[mine, :], sems.at[p]))
    for copy in copies:
        copy.wait()


def shaped(shape, dtype):
    return jax.ShapeDtypeStruct(shape, dtype)


def exchange(value, axes):
    return lax.all_to_all(value, axes, split_axis=0, concat_axis=0, tiled=True)


def exchange_sub(message):
    ring = lax.axis_size("sub")
    swapped = lax.ppermute(message[1], "sub", [(i, i ^ 1) for i in range(ring)])
    both = jnp.stack([message[0], swapped], axis=1)
    shifted = {}
    for ahead in (2, 1, 3):
        pairs = [(i, (i + 2 * ahead) % ring) for i in range(ring)]
        shifted[ahead] = lax.ppermute(both[ahead], "sub", pairs)
    return message, swapped, shifted[3], shifted[1], shifted[2]


def shards(
    beads,
    rot_perm,
    pool_ids,
    ball_counts,
    fine_qkv,
    fine_out,
    pool_weight,
    coarse_qkv,
    coarse_out,
    unpool_weight,
):
    own, channels = beads.shape
    both = ("leaf", "sub")
    subs = lax.axis_size("sub")
    devices = lax.axis_size("leaf") * subs
    bucket = own // devices
    nodes = own // 8
    wide = pool_weight.shape[1]
    size = wide // CHEADS
    wanted, slots = call(
        functools.partial(route_kernel, own=own, devices=devices),
        (shaped((devices, 128), jnp.int32), shaped((own // 128, 128), jnp.int32)),
        [vmem()],
        (vmem(), vmem()),
        flops=2 * devices * own * 256,
        nbytes=100000,
        name="route",
    )(rot_perm.reshape(own // 128, 128))
    requested = exchange(wanted.reshape(devices, 1, 128), both).reshape(devices, 128)
    places = call(
        functools.partial(place_kernel, nodes=nodes),
        shaped((own // 128, 128), jnp.int32),
        [vmem()],
        vmem(),
        flops=2 * nodes * own * 256,
        nbytes=20000,
        name="place",
    )(pool_ids.reshape(own // 128, 128))

    slots = slots.reshape(own)
    places = places.reshape(own)
    ball_flops = own * channels * channels * 8 + own * BALL * channels * 16

    after_tree = call(
        first_kernel,
        shaped((own, channels), F32),
        [hbm()] * 3,
        vmem(),
        [
            pltpu.VMEM((2, own // 2, channels), F32),
            pltpu.VMEM((channels, 3 * channels), BF16),
            pltpu.VMEM((channels, channels), BF16),
            pltpu.SemaphoreType.DMA((4,)),
        ],
        flops=ball_flops,
        nbytes=own * channels * 8,
        name="first",
    )(in_hbm(beads), in_hbm(fine_qkv), in_hbm(fine_out))
    answer, named = call(
        functools.partial(answer_kernel, bucket=bucket),
        (shaped((own, channels), BF16), shaped((own // 128, 128), jnp.int32)),
        [vmem(), vmem()],
        (vmem(), vmem()),
        [
            pltpu.VMEM((own, channels), F32),
            pltpu.SMEM((own // 128, 128), jnp.int32),
            pltpu.SemaphoreType.DMA(()),
        ],
        nbytes=own * channels * 6,
        name="answer",
    )(requested, after_tree)
    named = named.reshape(own)
    arrived = exchange(answer.reshape(devices, bucket, channels), both).reshape(own, channels)
    outgoing = call(
        second_kernel,
        shaped((own, channels), BF16),
        [smem()] + [vmem()] * 3,
        vmem(),
        [pltpu.VMEM((own, channels), F32)] * 2 + [pltpu.VMEM((BALL, channels), F32)] * 4,
        flops=ball_flops,
        nbytes=own * channels * 4,
        name="second",
    )(slots, arrived, fine_qkv, fine_out)
    coming = exchange(outgoing.reshape(devices, bucket, channels), both).reshape(own, channels)
    qkv_turned = coarse_qkv.transpose(0, 2, 1)
    out_turned = coarse_out.transpose(0, 2, 1)
    coming, qkv_turned, out_turned = lax.optimization_barrier((coming, qkv_turned, out_turned))
    message, features, placed = call(
        pool_kernel,
        (
            shaped((2, subs // 2, 3 * size, nodes), BF16),
            shaped((wide, nodes), F32),
            shaped((own, channels), F32),
        ),
        [smem(), smem(), vmem(), hbm(), vmem()],
        (vmem(), vmem(), vmem()),
        [
            pltpu.VMEM((own, channels), F32),
            pltpu.VMEM((own // 2, wide), BF16),
            pltpu.SemaphoreType.DMA(()),
        ],
        flops=2 * nodes * wide * (own // 2 + 3 * wide),
        nbytes=own * channels * 8,
        name="pool",
    )(named, places, coming, in_hbm(pool_weight), qkv_turned)
    for layer in range(2):
        received = exchange_sub(message)
        attended = call(
            coarse_kernel,
            shaped((2, subs // 2, size, nodes), BF16),
            [smem()] + [vmem()] * 5,
            vmem(),
            [pltpu.VMEM((subs, size, nodes), BF16), pltpu.VMEM((subs, nodes, size), BF16), pltpu.VMEM((subs, size + 16, nodes), BF16)]
            + [pltpu.VMEM((1, nodes), F32), pltpu.VMEM((size + 16, nodes), F32)],
            flops=subs * nodes * nodes * 3 * size * 4,
            nbytes=subs * nodes * size * 8,
            name="coarse",
        )(ball_counts, *received)
        back = exchange_sub(attended)
        if layer == 0:
            message, features = call(
                between_kernel,
                (shaped((2, subs // 2, 3 * size, nodes), BF16), shaped((wide, nodes), F32)),
                [vmem()] * 8,
                (vmem(), vmem()),
                [pltpu.VMEM((subs, size, nodes), BF16)],
                flops=2 * nodes * wide * 4 * wide,
                nbytes=nodes * wide * 8,
                name="between",
            )(*back, features, out_turned, qkv_turned)
    return call(
        last_kernel,
        shaped((own, channels), F32),
        [smem()] + [vmem()] * 9,
        hbm(),
        [
            pltpu.VMEM((own, channels), F32),
            pltpu.VMEM((own, channels), F32),
            pltpu.VMEM((subs, size, nodes), BF16),
            pltpu.SemaphoreType.DMA((4,)),
        ],
        flops=2 * nodes * wide * 3 * wide,
        nbytes=own * channels * 8,
        name="last",
    )(places, *back, features, out_turned, unpool_weight, placed)


def solution(mesh):
    placed = (
        P(("leaf", "sub"), None),
        P(("leaf", "sub")),
        P(("leaf", "sub")),
        P("leaf", None),
        P(),
        P(),
        P(),
        P(),
        P(),
        P(),
    )
    return jax.shard_map(
        shards, mesh=mesh, in_specs=placed, out_specs=P(("leaf", "sub"), None), check_vma=False
    )
```
